256 devices in a mesh: section: 4 (over x), dp: 2 (over core), expert: 32 (over z, y).
Axes of the slice: x: 4, y: 4, z: 8, core: 2. Of those that a mesh axis runs over, the one named last changes fastest.
Arguments:
- tokens: bfloat16 [4, 8192, 2048], P('section', ('dp', 'expert')), may hold values from -6 to 6
- out_grad: bfloat16 [4, 8192, 2048], P('section', ('dp', 'expert')), may hold values from -6 to 6
- expert_ids: int32 [4, 8192, 2], P('section', ('dp', 'expert')), may hold values from 0 to 31, all different within a row; in each aligned block of 128 rows (0 to 127, 128 to 255, ..., all dimensions but the last counted through in order) at most 16 rows name the same one
- route_probs: float32 [4, 8192, 2], P('section', ('dp', 'expert')), may hold values from 0.1 to 1
- gate_weight: bfloat16 [4, 32, 2048, 768], P('section', 'expert', None, 'dp'), may hold values from -0.125 to 0.125
- up_weight: bfloat16 [4, 32, 2048, 768], P('section', 'expert', None, 'dp'), may hold values from -0.125 to 0.125
- down_weight: bfloat16 [4, 32, 768, 2048], P('section', 'expert', 'dp'), may hold values from -0.21875 to 0.21875
Outputs:
- grad_in: bfloat16 [4, 8192, 2048], P('section', ('dp', 'expert'))
- prob_grad: float32 [4, 8192, 2], P('section', ('dp', 'expert'))
- gate_weight_grad: bfloat16 [4, 32, 2048, 768], P('section', 'expert', None, 'dp')
- up_weight_grad: bfloat16 [4, 32, 2048, 768], P('section', 'expert', None, 'dp')
- down_weight_grad: bfloat16 [4, 32, 768, 2048], P('section', 'expert', 'dp')
The draws below stay inside these ranges and needn't reach their ends.
Inputs may be any that keep to these rules, and one draw needn't show every extreme that they name: `expert_ids`: each token names 2 different experts; among the 128 tokens of one device (aligned blocks of 128 tokens of a section) no expert is named more than 16 times, a bound that some block reaches.
All inputs are finite; a program needn't handle non-finite values.
Results may differ from the reference program's by a relative error of at most 0.023.
Values may be sent and summed in bfloat16 or wider, within the bound.
A program may use at most 128 MiB of HBM per device.

```python
import math
import jax
import jax.numpy as jnp
import numpy as np
from jax import lax

D = 2048
FF = 768
TOP = 2
T_DEV = 128
SECTIONS = 4
EXPERTS = 32
TOKENS = 8192
CAP = 16
N_DP = 2


def block_levels(key, dims, pieces, smallest, top_value):
    factor_of = 1.0
    for position, parts in pieces:
        draws = jax.random.uniform(jax.random.fold_in(jax.random.fold_in(key, 6), position), (parts,), jnp.float32, smallest / len(pieces), top_value / len(pieces))
        factor_of = factor_of * jnp.repeat(jnp.exp(draws), dims[position] // parts).reshape((-1,) + (1,) * (len(dims) - 1 - position))
    return factor_of


def deal_out(own_key, own, number, rows, number_of, top, reach, skew):
    order = jax.random.permutation(own_key, number_of)
    packed, common = portions_of(number_of, rows * top, reach, skew, True), portions_of(number_of, rows * top, reach, skew, False)
    places = jnp.arange(number_of)

    def named(lengths, offset_by):
        used = int((lengths > 0).sum())
        fixed = max(1, used // 4)
        shifted = fixed + (places - fixed + offset_by * (used - fixed)) % max(1, number_of - fixed)
        return jnp.zeros((number_of,), jnp.int32).at[order[jnp.where(places < fixed, places, shifted)]].set(jnp.asarray(lengths, jnp.int32))

    lengths = jnp.where(number % 4 == 0, named(packed, number // 4), named(common, number - number // 4 - 1))
    mixed = jax.random.permutation(jax.random.fold_in(own, 3), number_of)
    source_of, receiver = mixed[0:number_of // 2 * 2:2], mixed[1:number_of // 2 * 2:2]
    room = jnp.minimum(lengths[source_of] - 1, reach - lengths[receiver]) // 2
    room = jnp.where((source_of == order[0]) | (receiver == order[0]) | (lengths[receiver] == 0), 0, jnp.maximum(room, 0))
    shifted = jax.random.randint(jax.random.fold_in(own, 4), (number_of // 2,), 0, 1 << 20) % (room + 1)
    lengths = lengths.at[source_of].add(-shifted).at[receiver].add(shifted)
    labels = jnp.searchsorted(jnp.cumsum(lengths), jnp.arange(rows * top), side="right").astype(jnp.int32)
    grid = labels.reshape(top, rows).T
    grid = grid[jax.random.permutation(jax.random.fold_in(own, 1), rows)]
    offset_by = jax.random.randint(jax.random.fold_in(own, 2), (rows, 1), 0, top)
    return jnp.take_along_axis(grid, (jnp.arange(top)[None, :] + offset_by) % top, axis=1)


def portions_of(amount, total, limit, lean, full):
    weights = [(1 << 20) // math.isqrt(standing ** lean) + 1 for standing in range(1, amount + 1)]
    largest = limit if full else min(limit, max(-(-total // amount), total * weights[0] // sum(weights)))
    least = 1 if total - largest >= amount - 1 else 0
    holding, rest = [largest] + [least] * (amount - 1), total - largest - least * (amount - 1)
    while rest > 0:
        movable = [i for i in range(1, amount) if holding[i] < largest] or [i for i in range(1, amount) if holding[i] < limit]
        mass, remaining = sum([weights[i] for i in movable]), rest
        for i in movable:
            extra = min(limit - holding[i], max(1, remaining * weights[i] // mass), rest)
            holding[i] = holding[i] + extra
            rest = rest - extra
    return np.array(holding)


def scatter_about(rng, extent, deviation, bound, cuts=(), kind=jnp.bfloat16):
    result = jax.random.normal(rng, extent, jnp.float32) * deviation
    if len(cuts) > 0:
        result = block_levels(rng, extent, cuts, -0.22, 0.18) * result
    return jnp.clip(result, min=-bound, max=bound).astype(kind)


def setup_inputs(seed: int = 0) -> dict:
    arg_keys = jax.random.split(jax.random.key(seed), 8)
    tokens = scatter_about(arg_keys[0], (SECTIONS, TOKENS, D), 1.0, 6.0, ((0, 4), (1, 64)))
    out_grad = scatter_about(arg_keys[1], (SECTIONS, TOKENS, D), 1.0, 6.0, ((0, 4), (1, 64)))
    expert_ids_keys = jax.random.split(jax.random.fold_in(arg_keys[2], 1), SECTIONS * TOKENS // T_DEV)
    expert_ids_turns = jax.random.permutation(jax.random.fold_in(arg_keys[2], 3), SECTIONS * TOKENS // T_DEV)
    expert_ids = jax.vmap(lambda own, number: deal_out(jax.random.fold_in(arg_keys[2], 2), own, number, T_DEV, EXPERTS, TOP, CAP, 2))(expert_ids_keys, expert_ids_turns).reshape((SECTIONS, TOKENS, TOP))
    route_probs = jnp.clip(0.1 + 0.9 * jax.random.uniform(arg_keys[3], (SECTIONS, TOKENS, TOP), jnp.float32) ** block_levels(arg_keys[3], (SECTIONS, TOKENS, TOP), ((0, 4), (1, 64)), -0.2, 0.2), 0.1, 1.0)
    gate_weight = scatter_about(arg_keys[4], (SECTIONS, EXPERTS, D, FF), D ** -0.5, 0.125, ((0, 4), (1, 32), (3, 2)))
    up_weight = scatter_about(arg_keys[5], (SECTIONS, EXPERTS, D, FF), D ** -0.5, 0.125, ((0, 4), (1, 32), (3, 2)))
    down_weight = scatter_about(arg_keys[6], (SECTIONS, EXPERTS, FF, D), FF ** -0.5, 0.21875, ((0, 4), (1, 32), (2, 2)))
    return dict(tokens=tokens, out_grad=out_grad, expert_ids=expert_ids, route_probs=route_probs, gate_weight=gate_weight, up_weight=up_weight, down_weight=down_weight)


def expert_grads(rows_in, grads_in, weights_in, gate_part, up_part, down_part):
    gate_pre = jnp.dot(rows_in, gate_part, preferred_element_type=jnp.float32)
    up_pre = jnp.dot(rows_in, up_part, preferred_element_type=jnp.float32)
    sigmoid_gate = jax.nn.sigmoid(gate_pre)
    activated = gate_pre * sigmoid_gate * up_pre
    scaled_act = (weights_in[:, None] * activated).astype(jnp.bfloat16)
    hidden_grad = jnp.dot(grads_in, down_part.T, preferred_element_type=jnp.float32)
    prob_part = jnp.sum(activated * hidden_grad, axis=1)
    hidden_scaled = weights_in[:, None] * hidden_grad
    gate_grad = (hidden_scaled * up_pre * sigmoid_gate * (1.0 + gate_pre * (1.0 - sigmoid_gate))).astype(jnp.bfloat16)
    up_grad = (hidden_scaled * gate_pre * sigmoid_gate).astype(jnp.bfloat16)
    route_dx = jnp.dot(gate_grad, gate_part.T, preferred_element_type=jnp.float32) + jnp.dot(up_grad, up_part.T, preferred_element_type=jnp.float32)
    grad_gate = jnp.dot(rows_in.T, gate_grad, preferred_element_type=jnp.float32)
    grad_up = jnp.dot(rows_in.T, up_grad, preferred_element_type=jnp.float32)
    grad_down = jnp.dot(scaled_act.T, grads_in, preferred_element_type=jnp.float32)
    return route_dx, prob_part, grad_gate, grad_up, grad_down


def reference(tokens, out_grad, expert_ids, route_probs, gate_weight, up_weight, down_weight):
    row_total = N_DP * EXPERTS * CAP
    token_grads, prob_grads, gate_list, up_list, down_list = [], [], [], [], []
    for section in range(SECTIONS):
        route_ids = expert_ids[section].reshape(-1)
        probs_flat = route_probs[section].reshape(-1)
        section_tokens = tokens[section]
        section_grads = out_grad[section]

        def one_expert(expert):
            hit = route_ids == expert
            picked = jnp.nonzero(hit, size=row_total, fill_value=0)[0].astype(jnp.int32)
            is_live = jnp.arange(row_total, dtype=jnp.int32) < jnp.sum(hit.astype(jnp.int32))
            token_index = picked // TOP
            zero_value = jnp.zeros((), jnp.bfloat16)
            rows_in = jnp.where(is_live[:, None], section_tokens[token_index], zero_value)
            grads_in = jnp.where(is_live[:, None], section_grads[token_index], zero_value)
            weights_in = jnp.where(is_live, probs_flat[picked], jnp.zeros((), jnp.float32))
            route_dx, prob_part, grad_gate, grad_up, grad_down = expert_grads(
                rows_in, grads_in, weights_in, gate_weight[section, expert], up_weight[section, expert], down_weight[section, expert])
            return (route_dx.astype(jnp.bfloat16), prob_part, grad_gate.astype(jnp.bfloat16),
                    grad_up.astype(jnp.bfloat16), grad_down.astype(jnp.bfloat16), picked, is_live)

        route_dx, prob_part, grad_gate, grad_up, grad_down, picked, is_live = lax.map(
            one_expert, jnp.arange(EXPERTS, dtype=jnp.int32))
        live_flat = is_live.reshape(-1)
        picked_flat = picked.reshape(-1)
        dx_flat = jnp.where(live_flat[:, None], route_dx.reshape(-1, D).astype(jnp.float32), jnp.zeros((), jnp.float32))
        summed = jnp.zeros((TOKENS * TOP, D), jnp.float32).at[picked_flat].add(dx_flat)
        token_grads.append(summed.reshape(TOKENS, TOP, D).sum(axis=1).astype(jnp.bfloat16))
        prob_flat = jnp.where(live_flat, prob_part.reshape(-1), jnp.zeros((), jnp.float32))
        prob_grads.append(jnp.zeros((TOKENS * TOP,), jnp.float32).at[picked_flat].add(prob_flat).reshape(TOKENS, TOP))
        gate_list.append(grad_gate)
        up_list.append(grad_up)
        down_list.append(grad_down)
    token_stack = jnp.stack(token_grads)
    grad_in = jnp.roll(token_stack, -1, axis=0)
    return grad_in, jnp.stack(prob_grads), jnp.stack(gate_list), jnp.stack(up_list), jnp.stack(down_list)
```

```python
import functools

import jax
import jax.numpy as jnp
from jax import lax
from jax.experimental import pallas as pl
from jax.experimental.pallas import tpu as pltpu
from jax.sharding import PartitionSpec as P

MESH = pl.DeviceIdType.MESH
NY = 4
NZ = 8
CAP = 16
ROWS = 128
SLOTS = NY * CAP
F32 = jnp.float32
BF16 = jnp.bfloat16
NT = (((1,), (1,)), ((), ()))
TN = (((0,), (0,)), ((), ()))


def block(direction, distance):
    if distance == 0:
        return 0
    if distance == 4:
        return 7
    return 2 * distance - 1 + direction


def row_base(b):
    if b == 0:
        return 0
    if b == 7:
        return SLOTS
    return ((b + 1) // 2) * 2 * SLOTS + ((b + 1) % 2) * SLOTS


def kernel(
    meta_ref, t_ref, g_ref, wg_hbm, wu_hbm, wd_hbm,
    gi_out, pg_out, og_out, ou_out, od_out,
    gt, gg, gm, tp, gp, pp, rt, rg, rp, wg, wu, wd,
    a_gate, a_up, a_act, dx, pr, yx, yp, sx, rx, sp, rpp, fin,
    wsg, wsu, wsd, wrg, wru, wrd, wog, wou, wod,
    ring_s, ring_r, meta_s, meta_r, disp_s, disp_r, back_s, back_r,
    red_s, red_r, redp_s, redp_r, fin_s, fin_r, w_l, w_s, w_r, wx_s, wx_r, wo_s,
):
    d_model = t_ref.shape[1]
    hid = wg_hbm.shape[1]
    full = 2 * hid
    me = lax.axis_index("expert")
    core = lax.axis_index("dp")
    sec = lax.axis_index("section")
    n_sec = lax.axis_size("section")
    y = lax.rem(me, NY)
    z = me // NY
    ring_to = ({"expert": lax.rem(z + 1, NZ) * NY + y}, {"expert": lax.rem(z + NZ - 1, NZ) * NY + y})
    y_to = [{"expert": z * NY + lax.rem(y + i, NY)} for i in range(NY)]
    twin = {"dp": 1 - core}
    x_prev = {"section": lax.rem(sec + n_sec - 1, n_sec)}
    x_next = {"section": lax.rem(sec + 1, n_sec)}
    pending = []

    def remote(src, dst, ssem, rsem, dev):
        return pltpu.make_async_remote_copy(
            src_ref=src, dst_ref=dst, send_sem=ssem, recv_sem=rsem, device_id=dev, device_id_type=MESH)

    def send(copy):
        copy.start()
        pending.append(copy)

    barrier = pltpu.get_barrier_semaphore()
    greet = [ring_to[0], ring_to[1], y_to[1], y_to[2], y_to[3], twin, x_prev, x_next]
    for dev in greet:
        pl.semaphore_signal(barrier, inc=1, device_id=dev, device_id_type=MESH)

    local_w = [
        pltpu.make_async_copy(wg_hbm, wg.at[:, pl.ds(0, hid)], w_l.at[0]),
        pltpu.make_async_copy(wu_hbm, wu.at[:, pl.ds(0, hid)], w_l.at[1]),
        pltpu.make_async_copy(wd_hbm, wd.at[pl.ds(0, hid)], w_l.at[2]),
    ]
    for copy in local_w:
        copy.start()

    ids = meta_ref[0:2, :]
    experts = lax.broadcasted_iota(jnp.int32, (NY * NZ, ROWS), 0).astype(F32)
    hit0 = jnp.where(experts == ids[0:1, :], 1.0, 0.0)
    hit1 = jnp.where(experts == ids[1:2, :], 1.0, 0.0)
    earlier = jnp.where(
        lax.broadcasted_iota(jnp.int32, (ROWS, ROWS), 0) < lax.broadcasted_iota(jnp.int32, (ROWS, ROWS), 1), 1.0, 0.0
    ).astype(BF16)
    before = jnp.dot((hit0 + hit1).astype(BF16), earlier, preferred_element_type=F32)
    slot0 = ids[0:1, :] * CAP + jnp.sum(hit0 * before, axis=0, keepdims=True)
    slot1 = ids[1:2, :] * CAP + jnp.sum(hit1 * before, axis=0, keepdims=True)
    gm[0] = jnp.concatenate([slot0, slot1, meta_ref[2:8, :]], axis=0)

    pl.semaphore_wait(barrier, len(greet))

    def meta_copy(d, k):
        src = gm.at[0] if k == 1 else gm.at[block(d, k - 1)]
        return remote(src, gm.at[block(d, k)], meta_s.at[d, k - 1], meta_r.at[d, k - 1], ring_to[d])

    def ring_copy(x, d, k):
        own, held = ((t_ref, gt), (g_ref, gg))[x]
        rows = pl.ds(d * (ROWS // 2), ROWS // 2) if k == 4 else pl.ds(0, ROWS)
        src = own.at[rows] if k == 1 else held.at[block(d, k - 1) - 1, rows]
        return remote(src, held.at[block(d, k) - 1, rows], ring_s.at[x, d, k - 1], ring_r.at[x, d, k - 1], ring_to[d])

    for d in range(2):
        send(meta_copy(d, 1))
    for x in range(2):
        for d in range(2):
            send(ring_copy(x, d, 1))
    w_copies = [
        remote(wg_hbm, wg.at[:, pl.ds(hid, hid)], w_s.at[0], w_r.at[0], twin),
        remote(wu_hbm, wu.at[:, pl.ds(hid, hid)], w_s.at[1], w_r.at[1], twin),
        remote(wd_hbm, wd.at[pl.ds(hid, hid)], w_s.at[2], w_r.at[2], twin),
    ]
    for copy in w_copies:
        send(copy)

    slot_row = lax.broadcasted_iota(jnp.int32, (SLOTS, ROWS), 0)
    target = ((z * NY + lax.rem(y + slot_row // CAP, NY)) * CAP + lax.rem(slot_row, CAP)).astype(F32)

    def one_hot(b):
        meta = gm[b]
        return meta[0:1, :] == target, meta[1:2, :] == target

    def disp_copy(b, i, x):
        staged, landed = ((tp, rt), (gp, rg), (pp, rp))[x]
        src = staged.at[b, pl.ds(i * CAP, CAP)]
        dst = landed.at[pl.ds(row_base(b) + (NY - i) * CAP, CAP)]
        return remote(src, dst, disp_s.at[b, i - 1, x], disp_r.at[b, i - 1, x], y_to[i])

    def pack(b, x):
        oh0, oh1 = one_hot(b)
        if x == 2:
            probs = gm[b]
            chosen = jnp.where(oh0, probs[2:3, :], 0.0) + jnp.where(oh1, probs[3:4, :], 0.0)
            spread = jnp.broadcast_to(jnp.sum(chosen, axis=1, keepdims=True), (SLOTS, ROWS))
            pp[b] = spread
            rp[row_base(b):row_base(b) + CAP, :] = spread[0:CAP, :]
        else:
            own, held, staged, landed = ((t_ref, gt, tp, rt), (g_ref, gg, gp, rg))[x]
            hot = (jnp.where(oh0, 1.0, 0.0) + jnp.where(oh1, 1.0, 0.0)).astype(BF16)
            rows = own[...] if b == 0 else held[b - 1]
            packed = jnp.dot(hot, rows, preferred_element_type=F32).astype(BF16)
            staged[b] = packed
            landed[row_base(b):row_base(b) + CAP, :] = packed[0:CAP, :]
        for i in range(1, NY):
            send(disp_copy(b, i, x))

    def landed(b):
        for i in range(1, NY):
            for x in range(3):
                disp_copy(b, i, x).wait_recv()

    def back_copy(b, i, x):
        src, dst = ((dx, yx), (pr, yp))[x]
        return remote(
            src.at[pl.ds(row_base(b) + (NY - i) * CAP, CAP)], dst.at[b, pl.ds(i * CAP, CAP)],
            back_s.at[b, i - 1, x], back_r.at[b, i - 1, x], y_to[NY - i])

    def chunk(c, blocks):
        rows = pl.ds(c * 2 * SLOTS, 2 * SLOTS)
        for b in blocks:
            landed(b)
        pr[rows, :] = jnp.zeros((2 * SLOTS, ROWS), F32)
        tile = 256

        @pl.loop(0, full // tile)
        def _(n):
            cols = pl.ds(pl.multiple_of(n * tile, tile), tile)
            tok = rt[rows, :]
            grd = rg[rows, :]
            gate = jnp.dot(tok, wg[:, cols], preferred_element_type=F32)
            up = jnp.dot(tok, wu[:, cols], preferred_element_type=F32)
            hidden = lax.dot_general(grd, wd[cols, :], NT, preferred_element_type=F32)
            prob = rp[rows, :][:, 0:1]
            sig = jax.nn.sigmoid(gate)
            silu = gate * sig
            act = silu * up
            a_act[rows, cols] = (prob * act).astype(BF16)
            pr[rows, :] += jnp.broadcast_to(jnp.sum(act * hidden, axis=1, keepdims=True), (2 * SLOTS, ROWS))
            scaled = prob * hidden
            a_gate[rows, cols] = (scaled * up * sig * (1.0 + gate * (1.0 - sig))).astype(BF16)
            a_up[rows, cols] = (scaled * silu).astype(BF16)

        tile_d = 512

        @pl.loop(0, d_model // tile_d)
        def _(n):
            cols = pl.ds(pl.multiple_of(n * tile_d, tile_d), tile_d)
            out = lax.dot_general(a_gate[rows, :], wg[cols, :], NT, preferred_element_type=F32)
            out += lax.dot_general(a_up[rows, :], wu[cols, :], NT, preferred_element_type=F32)
            dx[rows, cols] = out.astype(BF16)

        for b in blocks:
            for i in range(1, NY):
                for x in range(2):
                    send(back_copy(b, i, x))
            yx[b, 0:CAP, :] = dx[row_base(b):row_base(b) + CAP, :]
            yp[b, 0:CAP, :] = pr[row_base(b):row_base(b) + CAP, :]

    for x in (2, 0, 1):
        pack(0, x)
    for k in range(1, 4):
        for d in range(2):
            meta_copy(d, k).wait_recv()
            if k < 3 or d == 0:
                send(meta_copy(d, k + 1))
        for x in range(2):
            for d in range(2):
                ring_copy(x, d, k).wait_recv()
                send(ring_copy(x, d, k + 1))
        for d in range(2):
            for x in (2, 0, 1):
                pack(block(d, k), x)
        if k == 1:
            for copy in local_w:
                copy.wait()
            for copy in w_copies:
                copy.wait_recv()
        else:
            chunk(k - 1, (block(0, k - 1), block(1, k - 1)))
    meta_copy(0, 4).wait_recv()
    for d in range(2):
        ring_copy(0, d, 4).wait_recv()
    pack(7, 2)
    pack(7, 0)
    chunk(3, (block(0, 3), block(1, 3)))
    for d in range(2):
        ring_copy(1, d, 4).wait_recv()
    pack(7, 1)
    chunk(0, (0, 7))

    half_cols = d_model // 2
    half_rows = ROWS // 2

    def red_copy(d, m, s):
        rows = pl.ds(d * half_rows, half_rows) if m == 1 else pl.ds(0, ROWS)
        cols = pl.ds(s * half_cols, half_cols)
        return remote(
            sx.at[d, m - 1, rows, cols], rx.at[d, m - 1, rows, cols],
            red_s.at[d, m - 1, s], red_r.at[d, m - 1, s], ring_to[d])

    def redp_copy(d, m):
        return remote(sp.at[d, m - 1], rpp.at[d, m - 1], redp_s.at[d, m - 1], redp_r.at[d, m - 1], ring_to[d])

    def back_landed(b):
        for i in range(1, NY):
            for x in range(2):
                back_copy(b, i, x).wait_recv()

    def prob_part(b):
        oh0, oh1 = one_hot(b)
        val = yp[b]
        p0 = jnp.sum(jnp.where(oh0, val, 0.0), axis=0, keepdims=True)
        p1 = jnp.sum(jnp.where(oh1, val, 0.0), axis=0, keepdims=True)
        return jnp.concatenate([p0, p1, jnp.zeros((6, ROWS), F32)], axis=0)

    def spread_rows(b, s):
        oh0, oh1 = one_hot(b)
        hot = (jnp.where(oh0, 1.0, 0.0) + jnp.where(oh1, 1.0, 0.0)).astype(BF16)
        return lax.dot_general(hot, yx[b, :, s * half_cols:(s + 1) * half_cols], TN, preferred_element_type=F32)

    def stage(m):
        for d in range(2):
            b = block(1 - d, 5 - m)
            if m > 1 or d == 0:
                back_landed(b)
        for s in range(2):
            cols = slice(s * half_cols, (s + 1) * half_cols)
            for d in range(2):
                b = block(1 - d, 5 - m)
                part = spread_rows(b, s)
                if m == 1:
                    rows = slice(d * half_rows, (d + 1) * half_rows)
                    sx[d, 0, rows, cols] = part[rows].astype(BF16)
                else:
                    red_copy(d, m - 1, s).wait_recv()
                    if m == 2:
                        rows = slice(d * half_rows, (d + 1) * half_rows)
                        rest = slice((1 - d) * half_rows, (2 - d) * half_rows)
                        sx[d, 1, rows, cols] = (part[rows] + rx[d, 0, rows, cols].astype(F32)).astype(BF16)
                        sx[d, 1, rest, cols] = part[rest].astype(BF16)
                    else:
                        sx[d, m - 1, :, cols] = (part + rx[d, m - 2, :, cols].astype(F32)).astype(BF16)
                send(red_copy(d, m, s))
        for d in range(2):
            if m == 1 and d == 1:
                continue
            val = prob_part(block(1 - d, 5 - m))
            if m > 2 or (m == 2 and d == 0):
                redp_copy(d, m - 1).wait_recv()
                val = val + rpp[d, m - 2]
            sp[d, m - 1] = val
            send(redp_copy(d, m))

    tile = 256

    def grad_gate_up():
        @pl.loop(0, d_model // tile)
        def _(n):
            at = pl.ds(pl.multiple_of(n * tile, tile), tile)
            tok = rt[:, at]
            for acts, other, mine in ((a_gate, wsg, wog), (a_up, wsu, wou)):
                out = lax.dot_general(tok, acts[...], TN, preferred_element_type=F32).astype(BF16)
                mine[at, :] = out[:, 0:hid]
                other[at, :] = out[:, hid:full]

    def grad_down():
        @pl.loop(0, d_model // tile)
        def _(n):
            at = pl.ds(pl.multiple_of(n * tile, tile), tile)
            out = lax.dot_general(a_act[...], rg[:, at], TN, preferred_element_type=F32).astype(BF16)
            wod[:, at] = out[0:hid, :]
            wsd[:, at] = out[hid:full, :]

    trio = ((wsg, wrg, wog, og_out), (wsu, wru, wou, ou_out), (wsd, wrd, wod, od_out))

    def wx_copy(j):
        return remote(trio[j][0], trio[j][1], wx_s.at[j], wx_r.at[j], twin)

    def finish_weight(j):
        wx_copy(j).wait_recv()
        _, got, mine, out = trio[j]
        step = mine.shape[0] // 4

        @pl.loop(0, 4)
        def _(n):
            at = pl.ds(pl.multiple_of(n * step, step), step)
            mine[at, :] = (mine[at, :].astype(F32) + got[at, :].astype(F32)).astype(BF16)

        copy = pltpu.make_async_copy(mine, out, wo_s.at[j])
        copy.start()
        return copy

    stage(1)
    grad_gate_up()
    send(wx_copy(0))
    send(wx_copy(1))
    stage(2)
    grad_down()
    send(wx_copy(2))
    stage(3)
    outs = [finish_weight(0), finish_weight(1)]
    stage(4)
    outs.append(finish_weight(2))

    def fin_copy(s):
        cols = pl.ds(s * half_cols, half_cols)
        return remote(fin.at[:, cols], gi_out.at[:, cols], fin_s.at[s], fin_r.at[s], x_prev)

    back_landed(0)
    for s in range(2):
        cols = slice(s * half_cols, (s + 1) * half_cols)
        part = spread_rows(0, s)
        for d in range(2):
            red_copy(d, 4, s).wait_recv()
        part = part + rx[0, 3, :, cols].astype(F32) + rx[1, 3, :, cols].astype(F32)
        fin[:, cols] = part.astype(BF16)
        send(fin_copy(s))
    for d in range(2):
        redp_copy(d, 4).wait_recv()
    pg_out[...] = prob_part(0) + rpp[0, 3] + rpp[1, 3]
    for s in range(2):
        fin_copy(s).wait_recv()
    for copy in pending:
        copy.wait_send()
    for copy in outs:
        copy.wait()


def per_device(tokens, out_grad, expert_ids, route_probs, gate_weight, up_weight, down_weight):
    rows, d_model = tokens.shape[1:]
    hid = gate_weight.shape[3]
    full = 2 * hid
    meta = jnp.concatenate(
        [expert_ids[0].astype(F32).T, route_probs[0].T, jnp.zeros((4, rows), F32)], axis=0)
    vmem = pltpu.VMEM
    dma = pltpu.SemaphoreType.DMA
    in_vmem = pl.BlockSpec(memory_space=pltpu.VMEM)
    anywhere = pl.BlockSpec(memory_space=pl.ANY)
    n_slots = NZ * SLOTS
    scratch = [
        vmem((7, ROWS, d_model), BF16), vmem((7, ROWS, d_model), BF16), vmem((8, 8, ROWS), F32),
        vmem((8, SLOTS, d_model), BF16), vmem((8, SLOTS, d_model), BF16), vmem((8, SLOTS, ROWS), F32),
        vmem((n_slots, d_model), BF16), vmem((n_slots, d_model), BF16), vmem((n_slots, ROWS), F32),
        vmem((d_model, full), BF16), vmem((d_model, full), BF16), vmem((full, d_model), BF16),
        vmem((n_slots, full), BF16), vmem((n_slots, full), BF16), vmem((n_slots, full), BF16),
        vmem((n_slots, d_model), BF16), vmem((n_slots, ROWS), F32),
        vmem((8, SLOTS, d_model), BF16), vmem((8, SLOTS, ROWS), F32),
        vmem((2, 4, ROWS, d_model), BF16), vmem((2, 4, ROWS, d_model), BF16),
        vmem((2, 4, 8, ROWS), F32), vmem((2, 4, 8, ROWS), F32),
        vmem((ROWS, d_model), BF16),
        vmem((d_model, hid), BF16), vmem((d_model, hid), BF16), vmem((hid, d_model), BF16),
        vmem((d_model, hid), BF16), vmem((d_model, hid), BF16), vmem((hid, d_model), BF16),
        vmem((d_model, hid), BF16), vmem((d_model, hid), BF16), vmem((hid, d_model), BF16),
        dma((2, 2, 4)), dma((2, 2, 4)), dma((2, 4)), dma((2, 4)),
        dma((8, 3, 3)), dma((8, 3, 3)), dma((8, 3, 2)), dma((8, 3, 2)),
        dma((2, 4, 2)), dma((2, 4, 2)), dma((2, 4)), dma((2, 4)),
        dma((2,)), dma((2,)), dma((3,)), dma((3,)), dma((3,)), dma((3,)), dma((3,)), dma((3,)),
    ]
    grad_in, prob, grad_gate, grad_up, grad_down = pl.pallas_call(
        kernel,
        out_shape=(
            jax.ShapeDtypeStruct((rows, d_model), BF16), jax.ShapeDtypeStruct((8, rows), F32),
            jax.ShapeDtypeStruct((d_model, hid), BF16), jax.ShapeDtypeStruct((d_model, hid), BF16),
            jax.ShapeDtypeStruct((hid, d_model), BF16)),
        in_specs=[in_vmem, in_vmem, in_vmem, anywhere, anywhere, anywhere],
        out_specs=(anywhere, in_vmem, anywhere, anywhere, anywhere),
        scratch_shapes=scratch,
        compiler_params=pltpu.CompilerParams(
            collective_id=0, has_side_effects=True, vmem_limit_bytes=62 * 1024 * 1024),
    )(meta, tokens[0], out_grad[0], gate_weight[0, 0], up_weight[0, 0], down_weight[0, 0])
    return (
        grad_in[None], prob[0:2].T[None], grad_gate[None, None], grad_up[None, None], grad_down[None, None])


def solution(mesh):
    in_specs = (
        P("section", ("dp", "expert"), None), P("section", ("dp", "expert"), None),
        P("section", ("dp", "expert"), None), P("section", ("dp", "expert"), None),
        P("section", "expert", None, "dp"), P("section", "expert", None, "dp"), P("section", "expert", "dp", None))
    out_specs = (
        P("section", ("dp", "expert"), None), P("section", ("dp", "expert"), None),
        P("section", "expert", None, "dp"), P("section", "expert", None, "dp"), P("section", "expert", "dp", None))
    return jax.shard_map(per_device, mesh=mesh, in_specs=in_specs, out_specs=out_specs, check_vma=False)
```

```python
import jax
import jax.numpy as jnp
from jax import lax
from jax.experimental import pallas as pl
from jax.experimental.pallas import tpu as pltpu
from jax.sharding import PartitionSpec as P

MESH = pl.DeviceIdType.MESH
NY = 4
NZ = 8
CAP = 16
ROWS = 128
SLOTS = NY * CAP
HALF = SLOTS // 2
FAR = SLOTS + HALF
LAST = 3 * SLOTS
PARTS = 4
F32 = jnp.float32
BF16 = jnp.bfloat16
NT = (((1,), (1,)), ((), ()))
TN = (((0,), (0,)), ((), ()))


def block(direction, distance):
    if distance == 0:
        return 0
    if distance == 4:
        return 7
    return 2 * distance - 1 + direction


AHEAD = (0, block(1, 1))


def kernel(
    ids_ref, probs_ref, t_ref, g_ref, wg_hbm, wu_hbm, wd_hbm,
    gi_out, pg_out, og_out, ou_out, od_out,
    gt, gg, gm, gmx, tp, gp, pp, fs, fr, rt, rg, rp, wg, wu, wd,
    z_gate, z_up, a_gate, a_up, a_act, dx, pr, yx, yp, f1, f2, sx, rx, sp, rpp, fin,
    wsg, wsu, wsd, wrg, wru, wrd, wog, wou, wod,
    ring_s, ring_r, meta_s, meta_r, mx_s, mx_r, disp_s, disp_r, back_s, back_r,
    red_s, red_r, redp_s, redp_r, fin_s, w_l, w_s, w_r, wx_s, wx_r, wo_s,
):
    d_model = t_ref.shape[1]
    hid = wg_hbm.shape[1]
    full = 2 * hid
    me = lax.axis_index("expert")
    core = lax.axis_index("dp")
    sec = lax.axis_index("section")
    n_sec = lax.axis_size("section")
    y = lax.rem(me, NY)
    z = me // NY
    x_prev = lax.rem(sec + n_sec - 1, n_sec)
    x_next = lax.rem(sec + 1, n_sec)
    ring = (lax.rem(z + 1, NZ) * NY + y, lax.rem(z + NZ - 1, NZ) * NY + y)
    column = [z * NY + lax.rem(y + i, NY) for i in range(NY)]
    ring_to = [{"expert": e} for e in ring]
    ring_x = [{"section": x_prev, "expert": e} for e in ring]
    y_to = [{"expert": e} for e in column]
    y_x = [{"section": x_prev, "expert": e} for e in column]
    twin = {"dp": 1 - core}
    pending = []

    def remote(src, dst, ssem, rsem, dev):
        return pltpu.make_async_remote_copy(
            src_ref=src, dst_ref=dst, send_sem=ssem, recv_sem=rsem, device_id=dev, device_id_type=MESH)

    def send(copy):
        copy.start()
        pending.append(copy)

    barrier = pltpu.get_barrier_semaphore()
    greet = ring_to + y_to[1:] + [twin] + y_x + ring_x
    greet += [{"section": x_next, "expert": e} for e in column + list(ring)]
    for dev in greet:
        pl.semaphore_signal(barrier, inc=1, device_id=dev, device_id_type=MESH)

    local_w = [
        pltpu.make_async_copy(wg_hbm, wg.at[:, pl.ds(0, hid)], w_l.at[0]),
        pltpu.make_async_copy(wu_hbm, wu.at[:, pl.ds(0, hid)], w_l.at[1]),
        pltpu.make_async_copy(wd_hbm, wd.at[pl.ds(0, hid)], w_l.at[2]),
    ]
    for copy in local_w:
        copy.start()

    ids = ids_ref[...].astype(F32)
    experts = lax.broadcasted_iota(jnp.int32, (NY * NZ, ROWS), 0).astype(F32)
    hit0 = jnp.where(experts == ids[0:1, :], 1.0, 0.0)
    hit1 = jnp.where(experts == ids[1:2, :], 1.0, 0.0)
    earlier = jnp.where(
        lax.broadcasted_iota(jnp.int32, (ROWS, ROWS), 0) < lax.broadcasted_iota(jnp.int32, (ROWS, ROWS), 1), 1.0, 0.0
    ).astype(BF16)
    before = jnp.dot((hit0 + hit1).astype(BF16), earlier, preferred_element_type=F32)
    slot0 = ids[0:1, :] * CAP + jnp.sum(hit0 * before, axis=0, keepdims=True)
    slot1 = ids[1:2, :] * CAP + jnp.sum(hit1 * before, axis=0, keepdims=True)
    gm[0] = jnp.concatenate([slot0, slot1, probs_ref[...], jnp.zeros((4, ROWS), F32)], axis=0)

    pl.semaphore_wait(barrier, len(greet))

    def meta_copy(d, k):
        src = gm.at[0] if k == 1 else gm.at[block(d, k - 1)]
        return remote(src, gm.at[block(d, k)], meta_s.at[d, k - 1], meta_r.at[d, k - 1], ring_to[d])

    def metax_copy(j):
        return remote(gm.at[AHEAD[j]], gmx.at[j], mx_s.at[j], mx_r.at[j], {"section": x_prev})

    def ring_copy(x, d, k):
        own, held, staged = ((t_ref, gt, tp), (g_ref, gg, gp))[x]
        if k == 1:
            src, dst = own, held.at[block(d, 1) - 1]
        elif k == 2:
            src, dst = held.at[block(d, 1) - 1], held.at[block(d, 2) - 1]
        elif k == 3:
            src, dst = fs.at[x, d], fr.at[x, d]
        else:
            src, dst = fr.at[x, d, pl.ds(SLOTS, HALF)], staged.at[7, pl.ds(d * HALF, HALF)]
        return remote(src, dst, ring_s.at[x, d, k - 1], ring_r.at[x, d, k - 1], ring_to[d])

    for d in range(2):
        send(meta_copy(d, 1))
    for x in range(2):
        for d in range(2):
            send(ring_copy(x, d, 1))
    send(metax_copy(0))
    w_copies = [
        remote(wg_hbm, wg.at[:, pl.ds(hid, hid)], w_s.at[0], w_r.at[0], twin),
        remote(wu_hbm, wu.at[:, pl.ds(hid, hid)], w_s.at[1], w_r.at[1], twin),
        remote(wd_hbm, wd.at[pl.ds(hid, hid)], w_s.at[2], w_r.at[2], twin),
    ]
    for copy in w_copies:
        send(copy)

    def slot_names(plane, rows, first):
        row = lax.broadcasted_iota(jnp.int32, (rows, ROWS), 0)
        return ((plane * NY + lax.rem(y + first + row // CAP, NY)) * CAP + lax.rem(row, CAP)).astype(F32)

    def matches(meta, names):
        return meta[0:1, :] == names, meta[1:2, :] == names

    def as_hot(pair):
        return (jnp.where(pair[0], 1.0, 0.0) + jnp.where(pair[1], 1.0, 0.0)).astype(BF16)

    def near_hot(meta):
        return as_hot(matches(meta, slot_names(z, SLOTS, 0)))

    def far_hot(d):
        step = 1 if d == 0 else NZ - 1
        names = jnp.concatenate([
            slot_names(lax.rem(z + step, NZ), SLOTS, 0), slot_names(lax.rem(z + 2 * step, NZ), HALF, 2 * d)], axis=0)
        return as_hot(matches(gm[block(d, 2)], names))

    def staged_at(b, x):
        if x == 2:
            return pp.at[b]
        if b in (5, 6):
            return fr.at[x, b - 5]
        return (tp, gp)[x].at[b]

    def disp_copy(b, i, x):
        landing = (rt, rg, rp)[x]
        src = staged_at(b, x).at[pl.ds(i * CAP, CAP)]
        dst = landing.at[pl.ds(b * SLOTS + (NY - i) * CAP, CAP)]
        return remote(src, dst, disp_s.at[b, i - 1, x], disp_r.at[b, i - 1, x], y_to[i])

    def pack(b, x):
        top = slice(b * SLOTS, b * SLOTS + CAP)
        if x == 2:
            meta = gm[b]
            oh0, oh1 = matches(meta, slot_names(z, SLOTS, 0))
            chosen = jnp.where(oh0, meta[2:3, :], 0.0) + jnp.where(oh1, meta[3:4, :], 0.0)
            spread = jnp.broadcast_to(jnp.sum(chosen, axis=1, keepdims=True), (SLOTS, ROWS))
            pp[b] = spread
            rp[top, :] = spread[0:CAP, :]
        elif b < 5:
            own, held, staged, landing = ((t_ref, gt, tp, rt), (g_ref, gg, gp, rg))[x]
            rows = own[...] if b == 0 else held[b - 1]
            packed = jnp.dot(near_hot(gm[b]), rows, preferred_element_type=F32).astype(BF16)
            staged[b] = packed
            landing[top, :] = packed[0:CAP, :]
        for i in range(1, NY):
            send(disp_copy(b, i, x))
        if x < 2 and b >= 5:
            (rt, rg)[x][top, :] = staged_at(b, x)[0:CAP, :]

    def landed(b, x):
        for i in range(1, NY):
            disp_copy(b, i, x).wait_recv()

    def back_copy(b, i, x):
        rows = pl.ds(b * SLOTS + (0 if i == 0 else NY - i) * CAP, CAP)
        src, dst = ((dx, yx), (pr, yp))[x]
        dev = y_x[(NY - i) % NY] if x == 0 and b in AHEAD else y_to[(NY - i) % NY]
        return remote(src.at[rows], dst.at[b, pl.ds(i * CAP, CAP)], back_s.at[b, i, x], back_r.at[b, i, x], dev)

    def back_routes(b, x):
        return range(0 if x == 0 and b in AHEAD else 1, NY)

    def gate_up(first, count):
        tile = 256
        rows = pl.ds(first, count)

        @pl.loop(0, full // tile)
        def _(n):
            cols = pl.ds(pl.multiple_of(n * tile, tile), tile)
            tok = rt[rows, :]
            z_gate[0:count, cols] = jnp.dot(tok, wg[:, cols], preferred_element_type=F32)
            z_up[0:count, cols] = jnp.dot(tok, wu[:, cols], preferred_element_type=F32)

    def hidden_dx(first, count):
        tile = 256
        rows = pl.ds(first, count)
        pr[rows, :] = jnp.zeros((count, ROWS), F32)

        @pl.loop(0, full // tile)
        def _(n):
            cols = pl.ds(pl.multiple_of(n * tile, tile), tile)
            hidden = lax.dot_general(rg[rows, :], wd[cols, :], NT, preferred_element_type=F32)
            gate = z_gate[0:count, cols]
            up = z_up[0:count, cols]
            prob = rp[rows, :][:, 0:1]
            sig = jax.nn.sigmoid(gate)
            silu = gate * sig
            act = silu * up
            a_act[rows, cols] = (prob * act).astype(BF16)
            pr[rows, :] += jnp.broadcast_to(jnp.sum(act * hidden, axis=1, keepdims=True), (count, ROWS))
            scaled = prob * hidden
            a_gate[rows, cols] = (scaled * up * sig * (1.0 + gate * (1.0 - sig))).astype(BF16)
            a_up[rows, cols] = (scaled * silu).astype(BF16)

        tile_d = 512

        @pl.loop(0, d_model // tile_d)
        def _(n):
            cols = pl.ds(pl.multiple_of(n * tile_d, tile_d), tile_d)
            out = lax.dot_general(a_gate[rows, :], wg[cols, :], NT, preferred_element_type=F32)
            out += lax.dot_general(a_up[rows, :], wu[cols, :], NT, preferred_element_type=F32)
            dx[rows, cols] = out.astype(BF16)

    def send_back(blocks):
        for b in blocks:
            for x in range(2):
                for i in back_routes(b, x):
                    send(back_copy(b, i, x))
        for b in blocks:
            top = slice(b * SLOTS, b * SLOTS + CAP)
            if b not in AHEAD:
                yx[b, 0:CAP, :] = dx[top, :]
            yp[b, 0:CAP, :] = pr[top, :]

    def chunk(blocks):
        first, count = blocks[0] * SLOTS, len(blocks) * SLOTS
        for b in blocks:
            for x in (0, 1, 2):
                landed(b, x)
        gate_up(first, count)
        hidden_dx(first, count)
        send_back(blocks)

    for x in (2, 0, 1):
        pack(0, x)
    for d in range(2):
        meta_copy(d, 1).wait_recv()
        send(meta_copy(d, 2))
    for x in range(2):
        for d in range(2):
            ring_copy(x, d, 1).wait_recv()
            send(ring_copy(x, d, 2))
    send(metax_copy(1))
    for d in range(2):
        for x in (2, 0, 1):
            pack(block(d, 1), x)
    for copy in local_w:
        copy.wait()
    for copy in w_copies:
        copy.wait_recv()
    for d in range(2):
        meta_copy(d, 2).wait_recv()
        send(meta_copy(d, 3))
    for x in range(2):
        for d in range(2):
            ring_copy(x, d, 2).wait_recv()
            held = (gt, gg)[x]
            fs[x, d] = jnp.dot(far_hot(d), held[block(d, 2) - 1], preferred_element_type=F32).astype(BF16)
            send(ring_copy(x, d, 3))
        for d in range(2):
            if x == 0:
                pack(block(d, 2), 2)
            pack(block(d, 2), x)
        if x == 0:
            chunk((0, 1, 2))
    for d in range(2):
        meta_copy(d, 3).wait_recv()
        if d == 0:
            send(meta_copy(d, 4))
    for x in range(2):
        for d in range(2):
            ring_copy(x, d, 3).wait_recv()
            send(ring_copy(x, d, 4))
        for d in range(2):
            pack(block(d, 3), x)
        if x == 0:
            for d in range(2):
                pack(block(d, 3), 2)
            chunk((3, 4))
    meta_copy(0, 4).wait_recv()
    pack(7, 2)
    for x in range(2):
        for d in range(2):
            ring_copy(x, d, 4).wait_recv()
        pack(7, x)
    for b in (5, 6, 7):
        landed(b, 0)
    gate_up(5 * SLOTS, LAST)
    for b in (5, 6, 7):
        landed(b, 1)
        landed(b, 2)
    hidden_dx(5 * SLOTS, LAST)
    send_back((7, 5, 6))

    width = d_model // PARTS

    def red_copy(d, m, s):
        cols = pl.ds(s * width, width)
        dev = ring_to[d]
        if m == 0:
            src, dst = yx.at[7, pl.ds((1 - d) * HALF, HALF), cols], f1.at[d, :, cols]
        elif m == 1:
            src, dst = yx.at[block(1 - d, 3), :, cols], f2.at[d, pl.ds(0, SLOTS), cols]
        elif m == 2:
            src, dst = f1.at[d, :, cols], f2.at[d, pl.ds(SLOTS, HALF), cols]
        else:
            src, dst = sx.at[d, m - 3, :, cols], rx.at[d, m - 3, :, cols]
            if m == 3 + d:
                dev = ring_x[d]
        return remote(src, dst, red_s.at[d, m, s], red_r.at[d, m, s], dev)

    def redp_copy(d, m):
        return remote(sp.at[d, m - 1], rpp.at[d, m - 1], redp_s.at[d, m - 1], redp_r.at[d, m - 1], ring_to[d])

    def back_landed(b, x):
        for i in back_routes(b, x):
            back_copy(b, i, x).wait_recv()

    def prob_part(b):
        oh0, oh1 = matches(gm[b], slot_names(z, SLOTS, 0))
        val = yp[b]
        p0 = jnp.sum(jnp.where(oh0, val, 0.0), axis=0, keepdims=True)
        p1 = jnp.sum(jnp.where(oh1, val, 0.0), axis=0, keepdims=True)
        return jnp.concatenate([p0, p1, jnp.zeros((6, ROWS), F32)], axis=0)

    def prob_stage(m):
        for d in range(2):
            if m == 1 and d == 1:
                continue
            b = block(1 - d, 5 - m)
            back_landed(b, 1)
            val = prob_part(b)
            if m > 2 or (m == 2 and d == 0):
                redp_copy(d, m - 1).wait_recv()
                val = val + rpp[d, m - 2]
            sp[d, m - 1] = val
            send(redp_copy(d, m))

    def spread_rows(hot, rows):
        return lax.dot_general(hot, rows, TN, preferred_element_type=F32)

    tile = 256

    def grad_gate_up():
        @pl.loop(0, d_model // tile)
        def _(n):
            at = pl.ds(pl.multiple_of(n * tile, tile), tile)
            tok = rt[:, at]
            for acts, other, mine in ((a_gate, wsg, wog), (a_up, wsu, wou)):
                out = lax.dot_general(tok, acts[...], TN, preferred_element_type=F32).astype(BF16)
                mine[at, :] = out[:, 0:hid]
                other[at, :] = out[:, hid:full]

    def grad_down():
        @pl.loop(0, d_model // tile)
        def _(n):
            at = pl.ds(pl.multiple_of(n * tile, tile), tile)
            out = lax.dot_general(a_act[...], rg[:, at], TN, preferred_element_type=F32).astype(BF16)
            wod[:, at] = out[0:hid, :]
            wsd[:, at] = out[hid:full, :]

    trio = ((wsg, wrg, wog, og_out), (wsu, wru, wou, ou_out), (wsd, wrd, wod, od_out))
    outs = []

    def wx_copy(j):
        return remote(trio[j][0], trio[j][1], wx_s.at[j], wx_r.at[j], twin)

    def finish_weight(j):
        wx_copy(j).wait_recv()
        _, got, mine, out = trio[j]
        step = mine.shape[0] // 4

        @pl.loop(0, 4)
        def _(n):
            at = pl.ds(pl.multiple_of(n * step, step), step)
            mine[at, :] = (mine[at, :].astype(F32) + got[at, :].astype(F32)).astype(BF16)

        copy = pltpu.make_async_copy(mine, out, wo_s.at[j])
        copy.start()
        outs.append(copy)

    back_landed(7, 0)
    for d in range(2):
        for s in range(PARTS):
            send(red_copy(d, 0, s))
    for d in range(2):
        back_landed(block(1 - d, 3), 0)
        for s in range(PARTS):
            send(red_copy(d, 1, s))
    prob_stage(1)
    grad_gate_up()
    send(wx_copy(0))
    send(wx_copy(1))
    for s in range(PARTS):
        for d in range(2):
            red_copy(d, 0, s).wait_recv()
            send(red_copy(d, 2, s))
    prob_stage(2)
    grad_down()
    send(wx_copy(2))
    for d in range(2):
        back_landed(block(1 - d, 2), 0)
    for s in range(PARTS):
        cols = slice(s * width, (s + 1) * width)
        for d in range(2):
            b = block(1 - d, 2)
            part = spread_rows(near_hot(gm[b]), yx[b, :, cols])
            red_copy(d, 1, s).wait_recv()
            red_copy(d, 2, s).wait_recv()
            part = part + spread_rows(far_hot(1 - d), f2[d, :, cols])
            sx[d, 0, :, cols] = part.astype(BF16)
            send(red_copy(d, 3, s))
    prob_stage(3)
    finish_weight(0)
    for j in range(2):
        metax_copy(j).wait_recv()
    for d in range(2):
        back_landed(block(1 - d, 1), 0)
    for s in range(PARTS):
        cols = slice(s * width, (s + 1) * width)
        for d in range(2):
            b = block(1 - d, 1)
            meta = gmx[1] if d == 0 else gm[b]
            part = spread_rows(near_hot(meta), yx[b, :, cols])
            red_copy(d, 3, s).wait_recv()
            sx[d, 1, :, cols] = (part + rx[d, 0, :, cols].astype(F32)).astype(BF16)
            send(red_copy(d, 4, s))
    prob_stage(4)
    finish_weight(1)
    finish_weight(2)
    back_landed(0, 0)
    back_landed(0, 1)
    for s in range(PARTS):
        cols = slice(s * width, (s + 1) * width)
        part = spread_rows(near_hot(gmx[0]), yx[0, :, cols])
        for d in range(2):
            red_copy(d, 4, s).wait_recv()
        part = part + rx[0, 1, :, cols].astype(F32) + rx[1, 1, :, cols].astype(F32)
        fin[:, cols] = part.astype(BF16)
        at = pl.ds(s * width, width)
        copy = pltpu.make_async_copy(fin.at[:, at], gi_out.at[:, at], fin_s.at[s])
        copy.start()
        outs.append(copy)
    for d in range(2):
        redp_copy(d, 4).wait_recv()
    pg_out[...] = (prob_part(0) + rpp[0, 3] + rpp[1, 3])[0:2, :]
    for copy in pending:
        copy.wait_send()
    for copy in outs:
        copy.wait()


def hand_over(gi, pg, og, ou, od, gi_out, pg_out, og_out, ou_out, od_out, b_gi, b_og, b_ou, b_od, in_sem, out_sem):
    pg_out[...] = pg[...]
    pieces = []
    for src, held, dst in ((gi, b_gi, gi_out), (og, b_og, og_out), (ou, b_ou, ou_out), (od, b_od, od_out)):
        step = max(src.shape[0] // 4, 128)
        for first in range(0, src.shape[0], step):
            rows = pl.ds(first, step)
            pieces.append((src.at[rows], held.at[rows], dst.at[rows]))
    loads = [pltpu.make_async_copy(p[0], p[1], in_sem.at[j]) for j, p in enumerate(pieces)]
    stores = [pltpu.make_async_copy(p[1], p[2], out_sem.at[j]) for j, p in enumerate(pieces)]
    for copy in loads:
        copy.start()
    for load, store in zip(loads, stores):
        load.wait()
        store.start()
    for copy in stores:
        copy.wait()


def per_device(tokens, out_grad, expert_ids, route_probs, gate_weight, up_weight, down_weight):
    rows, d_model = tokens.shape[1:]
    hid = gate_weight.shape[3]
    full = 2 * hid
    vmem = pltpu.VMEM
    dma = pltpu.SemaphoreType.DMA
    in_vmem = pl.BlockSpec(memory_space=pltpu.VMEM)
    anywhere = pl.BlockSpec(memory_space=pl.ANY)
    n_slots = NZ * SLOTS
    scratch = [
        vmem((4, ROWS, d_model), BF16), vmem((4, ROWS, d_model), BF16), vmem((8, 8, ROWS), F32), vmem((2, 8, ROWS), F32),
        vmem((8, SLOTS, d_model), BF16), vmem((8, SLOTS, d_model), BF16), vmem((8, SLOTS, ROWS), F32),
        vmem((2, 2, FAR, d_model), BF16), vmem((2, 2, FAR, d_model), BF16),
        vmem((n_slots, d_model), BF16), vmem((n_slots, d_model), BF16), vmem((n_slots, ROWS), F32),
        vmem((d_model, full), BF16), vmem((d_model, full), BF16), vmem((full, d_model), BF16),
        vmem((LAST, full), F32), vmem((LAST, full), F32),
        vmem((n_slots, full), BF16), vmem((n_slots, full), BF16), vmem((n_slots, full), BF16),
        vmem((n_slots, d_model), BF16), vmem((n_slots, ROWS), F32),
        vmem((8, SLOTS, d_model), BF16), vmem((8, SLOTS, ROWS), F32),
        vmem((2, HALF, d_model), BF16), vmem((2, FAR, d_model), BF16),
        vmem((2, 2, ROWS, d_model), BF16), vmem((2, 2, ROWS, d_model), BF16),
        vmem((2, 4, 8, ROWS), F32), vmem((2, 4, 8, ROWS), F32),
        vmem((ROWS, d_model), BF16),
        vmem((d_model, hid), BF16), vmem((d_model, hid), BF16), vmem((hid, d_model), BF16),
        vmem((d_model, hid), BF16), vmem((d_model, hid), BF16), vmem((hid, d_model), BF16),
        vmem((d_model, hid), BF16), vmem((d_model, hid), BF16), vmem((hid, d_model), BF16),
        dma((2, 2, 4)), dma((2, 2, 4)), dma((2, 4)), dma((2, 4)), dma((2,)), dma((2,)),
        dma((8, 3, 3)), dma((8, 3, 3)), dma((8, 4, 2)), dma((8, 4, 2)),
        dma((2, 5, PARTS)), dma((2, 5, PARTS)), dma((2, 4)), dma((2, 4)),
        dma((PARTS,)), dma((3,)), dma((3,)), dma((3,)), dma((3,)), dma((3,)), dma((3,)),
    ]
    shapes = (
        jax.ShapeDtypeStruct((rows, d_model), BF16), jax.ShapeDtypeStruct((2, rows), F32),
        jax.ShapeDtypeStruct((d_model, hid), BF16), jax.ShapeDtypeStruct((d_model, hid), BF16),
        jax.ShapeDtypeStruct((hid, d_model), BF16))
    results = pl.pallas_call(
        kernel,
        out_shape=shapes,
        in_specs=[in_vmem, in_vmem, in_vmem, in_vmem, anywhere, anywhere, anywhere],
        out_specs=(anywhere, in_vmem, anywhere, anywhere, anywhere),
        scratch_shapes=scratch,
        compiler_params=pltpu.CompilerParams(
            collective_id=0, has_side_effects=True, vmem_limit_bytes=62 * 1024 * 1024),
    )(expert_ids[0].T, route_probs[0].T, tokens[0], out_grad[0], gate_weight[0, 0], up_weight[0, 0], down_weight[0, 0])
    grad_in, prob, grad_gate, grad_up, grad_down = pl.pallas_call(
        hand_over,
        out_shape=shapes,
        in_specs=[anywhere, in_vmem, anywhere, anywhere, anywhere],
        out_specs=(anywhere, in_vmem, anywhere, anywhere, anywhere),
        scratch_shapes=[
            vmem((rows, d_model), BF16), vmem((d_model, hid), BF16), vmem((d_model, hid), BF16), vmem((hid, d_model), BF16),
            dma((16,)), dma((16,))],
    )(*results)
    return (
        grad_in[None], prob.T[None], grad_gate[None, None], grad_up[None, None], grad_down[None, None])


def solution(mesh):
    in_specs = (
        P("section", ("dp", "expert"), None), P("section", ("dp", "expert"), None),
        P("section", ("dp", "expert"), None), P("section", ("dp", "expert"), None),
        P("section", "expert", None, "dp"), P("section", "expert", None, "dp"), P("section", "expert", "dp", None))
    out_specs = (
        P("section", ("dp", "expert"), None), P("section", ("dp", "expert"), None),
        P("section", "expert", None, "dp"), P("section", "expert", None, "dp"), P("section", "expert", "dp", None))
    return jax.shard_map(per_device, mesh=mesh, in_specs=in_specs, out_specs=out_specs, check_vma=False)
```

```python
import jax
import jax.numpy as jnp
from jax import lax
from jax.experimental import pallas as pl
from jax.experimental.pallas import tpu as pltpu
from jax.sharding import PartitionSpec as P

MESH = pl.DeviceIdType.MESH
NY = 4
NZ = 8
CAP = 16
ROWS = 128
SLOTS = NY * CAP
HALF = SLOTS // 2
FAR = SLOTS + HALF
LAST = 3 * SLOTS
PARTS = 4
F32 = jnp.float32
BF16 = jnp.bfloat16
NT = (((1,), (1,)), ((), ()))
TN = (((0,), (0,)), ((), ()))


def block(direction, distance):
    if distance == 0:
        return 0
    if distance == 4:
        return 7
    return 2 * distance - 1 + direction


AHEAD = (0, block(1, 1))


def kernel(
    ids_ref, probs_ref, t_hbm, g_hbm, wg_hbm, wu_hbm, wd_hbm,
    gi_out, pg_out, og_out, ou_out, od_out,
    t_ref, g_ref, gt, gg, gm, gmx, tp, gp, pp, fs, fr, rt, rg, rp, wg, wu, wd,
    wgt, wut, wdt,
    z_gate, z_up, a_gate, a_up, a_act, dx, pr, yx, yp, f1, f2, sx, rx, sp, rpp,
    wrg, wru, wrd,
    ring_s, ring_r, meta_s, meta_r, mx_s, mx_r, disp_s, disp_r, back_s, back_r, part_s, part_r,
    red_s, red_r, redp_s, redp_r, x_l, w_l, w_s, w_r, wx_s, wx_r,
):
    d_model = t_hbm.shape[1]
    hid = wg_hbm.shape[1]
    full = 2 * hid
    me = lax.axis_index("expert")
    core = lax.axis_index("dp")
    sec = lax.axis_index("section")
    n_sec = lax.axis_size("section")
    y = lax.rem(me, NY)
    z = me // NY
    x_prev = lax.rem(sec + n_sec - 1, n_sec)
    x_next = lax.rem(sec + 1, n_sec)
    ring = (lax.rem(z + 1, NZ) * NY + y, lax.rem(z + NZ - 1, NZ) * NY + y)
    column = [z * NY + lax.rem(y + i, NY) for i in range(NY)]
    ring_to = [{"expert": e} for e in ring]
    ring_x = [{"section": x_prev, "expert": e} for e in ring]
    y_to = [{"expert": e} for e in column]
    y_x = [{"section": x_prev, "expert": e} for e in column]
    twin = {"dp": 1 - core}
    pending = []

    def remote(src, dst, ssem, rsem, dev):
        return pltpu.make_async_remote_copy(
            src_ref=src, dst_ref=dst, send_sem=ssem, recv_sem=rsem, device_id=dev, device_id_type=MESH)

    def send(copy):
        copy.start()
        pending.append(copy)

    barrier = pltpu.get_barrier_semaphore()
    greet = ring_to + y_to[1:] + [twin] + y_x + ring_x
    greet += [{"section": x_next, "expert": e} for e in column + list(ring)]
    for dev in greet:
        pl.semaphore_signal(barrier, inc=1, device_id=dev, device_id_type=MESH)

    local_w = [
        pltpu.make_async_copy(wg_hbm, wg.at[:, pl.ds(0, hid)], w_l.at[0]),
        pltpu.make_async_copy(wu_hbm, wu.at[:, pl.ds(0, hid)], w_l.at[1]),
        pltpu.make_async_copy(wd_hbm, wd.at[pl.ds(0, hid)], w_l.at[2]),
    ]
    for copy in local_w:
        copy.start()

    local_x = [pltpu.make_async_copy(t_hbm, t_ref, x_l.at[0]), pltpu.make_async_copy(g_hbm, g_ref, x_l.at[1])]
    for copy in local_x:
        copy.start()

    pl.semaphore_wait(barrier, len(greet))

    def meta_copy(d, k):
        src = gm.at[0] if k == 1 else gm.at[block(d, k - 1)]
        return remote(src, gm.at[block(d, k)], meta_s.at[d, k - 1], meta_r.at[d, k - 1], ring_to[d])

    def metax_copy(j):
        return remote(gm.at[AHEAD[j]], gmx.at[j], mx_s.at[j], mx_r.at[j], {"section": x_prev})

    def ring_copy(x, d, k):
        own, held, staged = ((t_hbm, gt, tp), (g_hbm, gg, gp))[x]
        if k == 1:
            src, dst = own, held.at[block(d, 1) - 1]
        elif k == 2:
            src, dst = held.at[block(d, 1) - 1], held.at[block(d, 2) - 1]
        elif k == 3:
            src, dst = fs.at[x, d], fr.at[x, d]
        else:
            src, dst = fr.at[x, d, pl.ds(SLOTS, HALF)], staged.at[7, pl.ds(d * HALF, HALF)]
        return remote(src, dst, ring_s.at[x, d, k - 1], ring_r.at[x, d, k - 1], ring_to[d])

    for d in range(2):
        send(ring_copy(0, d, 1))

    ids = ids_ref[...].astype(F32)
    experts = lax.broadcasted_iota(jnp.int32, (NY * NZ, ROWS), 0).astype(F32)
    hit0 = jnp.where(experts == ids[0:1, :], 1.0, 0.0)
    hit1 = jnp.where(experts == ids[1:2, :], 1.0, 0.0)
    earlier = jnp.where(
        lax.broadcasted_iota(jnp.int32, (ROWS, ROWS), 0) < lax.broadcasted_iota(jnp.int32, (ROWS, ROWS), 1), 1.0, 0.0
    ).astype(BF16)
    before = jnp.dot((hit0 + hit1).astype(BF16), earlier, preferred_element_type=F32)
    slot0 = ids[0:1, :] * CAP + jnp.sum(hit0 * before, axis=0, keepdims=True)
    slot1 = ids[1:2, :] * CAP + jnp.sum(hit1 * before, axis=0, keepdims=True)
    gm[0] = jnp.concatenate([slot0, slot1, probs_ref[...], jnp.zeros((4, ROWS), F32)], axis=0)

    for d in range(2):
        send(meta_copy(d, 1))
    for d in range(2):
        send(ring_copy(1, d, 1))
    send(metax_copy(0))
    w_copies = [
        remote(wg_hbm, wg.at[:, pl.ds(hid, hid)], w_s.at[0], w_r.at[0], twin),
        remote(wu_hbm, wu.at[:, pl.ds(hid, hid)], w_s.at[1], w_r.at[1], twin),
        remote(wd_hbm, wd.at[pl.ds(hid, hid)], w_s.at[2], w_r.at[2], twin),
    ]
    for copy in w_copies:
        send(copy)

    def slot_names(plane, rows, first):
        row = lax.broadcasted_iota(jnp.int32, (rows, ROWS), 0)
        return ((plane * NY + lax.rem(y + first + row // CAP, NY)) * CAP + lax.rem(row, CAP)).astype(F32)

    def matches(meta, names):
        return meta[0:1, :] == names, meta[1:2, :] == names

    def as_hot(pair):
        return (jnp.where(pair[0], 1.0, 0.0) + jnp.where(pair[1], 1.0, 0.0)).astype(BF16)

    def near_hot(meta):
        return as_hot(matches(meta, slot_names(z, SLOTS, 0)))

    def far_hot(d):
        step = 1 if d == 0 else NZ - 1
        names = jnp.concatenate([
            slot_names(lax.rem(z + step, NZ), SLOTS, 0), slot_names(lax.rem(z + 2 * step, NZ), HALF, 2 * d)], axis=0)
        return as_hot(matches(gm[block(d, 2)], names))

    def staged_at(b, x):
        if x == 2:
            return pp.at[b]
        if b in (5, 6):
            return fr.at[x, b - 5]
        return (tp, gp)[x].at[b]

    def disp_copy(b, i, x):
        landing = (rt, rg, rp)[x]
        src = staged_at(b, x).at[pl.ds(i * CAP, CAP)]
        dst = landing.at[pl.ds(b * SLOTS + (NY - i) * CAP, CAP)]
        return remote(src, dst, disp_s.at[b, i - 1, x], disp_r.at[b, i - 1, x], y_to[i])

    def pack(b, x):
        top = slice(b * SLOTS, b * SLOTS + CAP)
        if x == 2:
            meta = gm[b]
            oh0, oh1 = matches(meta, slot_names(z, SLOTS, 0))
            chosen = jnp.where(oh0, meta[2:3, :], 0.0) + jnp.where(oh1, meta[3:4, :], 0.0)
            spread = jnp.broadcast_to(jnp.sum(chosen, axis=1, keepdims=True), (SLOTS, ROWS))
            pp[b] = spread
            rp[top, :] = spread[0:CAP, :]
        elif b < 5:
            own, held, staged, landing = ((t_ref, gt, tp, rt), (g_ref, gg, gp, rg))[x]
            rows = own[...] if b == 0 else held[b - 1]
            packed = jnp.dot(near_hot(gm[b]), rows, preferred_element_type=F32).astype(BF16)
            staged[b] = packed
            landing[top, :] = packed[0:CAP, :]
        for i in range(1, NY):
            send(disp_copy(b, i, x))
        if x < 2 and b >= 5:
            (rt, rg)[x][top, :] = staged_at(b, x)[0:CAP, :]

    def landed(b, x):
        for i in range(1, NY):
            disp_copy(b, i, x).wait_recv()

    def back_copy(b, i, x):
        rows = pl.ds(b * SLOTS + (0 if i == 0 else NY - i) * CAP, CAP)
        src, dst = ((dx, yx), (pr, yp))[x]
        dev = y_x[(NY - i) % NY] if x == 0 and b in AHEAD else y_to[(NY - i) % NY]
        return remote(src.at[rows], dst.at[b, pl.ds(i * CAP, CAP)], back_s.at[b, i, x], back_r.at[b, i, x], dev)

    def back_routes(b, x):
        return range(0 if x == 0 and b in AHEAD else 1, NY)

    def gate_up(first, count):
        tile = 256
        rows = pl.ds(first, count)

        @pl.loop(0, full // tile)
        def _(n):
            cols = pl.ds(pl.multiple_of(n * tile, tile), tile)
            tok = rt[rows, :]
            z_gate[0:count, cols] = jnp.dot(tok, wg[:, cols], preferred_element_type=F32)
            z_up[0:count, cols] = jnp.dot(tok, wu[:, cols], preferred_element_type=F32)

    def activations(first, count):
        tile = 256
        rows = pl.ds(first, count)
        pr[rows, :] = jnp.zeros((count, ROWS), F32)

        @pl.loop(0, full // tile)
        def _(n):
            cols = pl.ds(pl.multiple_of(n * tile, tile), tile)
            hidden = jnp.dot(rg[rows, :], wdt[:, cols], preferred_element_type=F32)
            gate = z_gate[0:count, cols]
            up = z_up[0:count, cols]
            prob = rp[rows, :][:, 0:1]
            sig = jax.nn.sigmoid(gate)
            silu = gate * sig
            act = silu * up
            a_act[rows, cols] = (prob * act).astype(BF16)
            pr[rows, :] += jnp.broadcast_to(jnp.sum(act * hidden, axis=1, keepdims=True), (count, ROWS))
            scaled = prob * hidden
            a_gate[rows, cols] = (scaled * up * sig * (1.0 + gate * (1.0 - sig))).astype(BF16)
            a_up[rows, cols] = (scaled * silu).astype(BF16)

    width = d_model // PARTS

    def dx_part(first, count, part):
        rows = pl.ds(first, count)
        cols = pl.ds(part * width, width) if isinstance(part, int) else pl.ds(pl.multiple_of(part * width, width), width)
        out = jnp.dot(a_gate[rows, :], wgt[:, cols], preferred_element_type=F32)
        out += jnp.dot(a_up[rows, :], wut[:, cols], preferred_element_type=F32)
        dx[rows, cols] = out.astype(BF16)

    def part_copy(b, i, part):
        cols = pl.ds(part * width, width)
        return remote(
            dx.at[pl.ds(b * SLOTS + (NY - i) * CAP, CAP), cols], yx.at[b, pl.ds(i * CAP, CAP), cols],
            part_s.at[b - 5, i - 1, part], part_r.at[b - 5, i - 1, part], y_to[NY - i])

    def send_back(blocks):
        for b in blocks:
            for x in range(2):
                for i in back_routes(b, x):
                    send(back_copy(b, i, x))
        for b in blocks:
            top = slice(b * SLOTS, b * SLOTS + CAP)
            if b not in AHEAD:
                yx[b, 0:CAP, :] = dx[top, :]
            yp[b, 0:CAP, :] = pr[top, :]

    def chunk(blocks):
        first, count = blocks[0] * SLOTS, len(blocks) * SLOTS
        for b in blocks:
            for x in (0, 1, 2):
                landed(b, x)
        gate_up(first, count)
        activations(first, count)

        @pl.loop(0, PARTS)
        def _(part):
            dx_part(first, count, part)

        send_back(blocks)

    for copy in local_x:
        copy.wait()
    for x in (2, 0, 1):
        pack(0, x)
    for d in range(2):
        meta_copy(d, 1).wait_recv()
        send(meta_copy(d, 2))
    for x in range(2):
        for d in range(2):
            ring_copy(x, d, 1).wait_recv()
            send(ring_copy(x, d, 2))
    send(metax_copy(1))
    for d in range(2):
        for x in (2, 0, 1):
            pack(block(d, 1), x)
    for copy in local_w:
        copy.wait()
    for copy in w_copies:
        copy.wait_recv()

    @pl.loop(0, full // 256)
    def _(n):
        at = pl.ds(pl.multiple_of(n * 256, 256), 256)
        wdt[:, at] = wd[at, :].T

    @pl.loop(0, d_model // 256)
    def _(n):
        at = pl.ds(pl.multiple_of(n * 256, 256), 256)
        wgt[:, at] = wg[at, :].T
        wut[:, at] = wu[at, :].T

    for d in range(2):
        meta_copy(d, 2).wait_recv()
        send(meta_copy(d, 3))
    for x in range(2):
        for d in range(2):
            ring_copy(x, d, 2).wait_recv()
            held = (gt, gg)[x]
            fs[x, d] = jnp.dot(far_hot(d), held[block(d, 2) - 1], preferred_element_type=F32).astype(BF16)
            send(ring_copy(x, d, 3))
        for d in range(2):
            if x == 0:
                pack(block(d, 2), 2)
            pack(block(d, 2), x)
        if x == 0:
            chunk((0, 1, 2))
    for d in range(2):
        meta_copy(d, 3).wait_recv()
        if d == 0:
            send(meta_copy(d, 4))
    for x in range(2):
        for d in range(2):
            ring_copy(x, d, 3).wait_recv()
            send(ring_copy(x, d, 4))
        for d in range(2):
            pack(block(d, 3), x)
        if x == 0:
            for d in range(2):
                pack(block(d, 3), 2)
            chunk((3, 4))
    meta_copy(0, 4).wait_recv()
    pack(7, 2)
    for x in range(2):
        for d in range(2):
            ring_copy(x, d, 4).wait_recv()
        pack(7, x)
    for b in (5, 6, 7):
        landed(b, 0)
    gate_up(5 * SLOTS, LAST)
    for b in (5, 6, 7):
        landed(b, 1)
        landed(b, 2)
    activations(5 * SLOTS, LAST)
    for b in (7, 5, 6):
        for i in range(1, NY):
            send(back_copy(b, i, 1))
        yp[b, 0:CAP, :] = pr[b * SLOTS:b * SLOTS + CAP, :]
    for part in range(PARTS):
        dx_part(5 * SLOTS, LAST, part)
        for b in (7, 5, 6):
            for i in range(1, NY):
                send(part_copy(b, i, part))
        for b in (7, 5, 6):
            top, cols = slice(b * SLOTS, b * SLOTS + CAP), slice(part * width, (part + 1) * width)
            yx[b, 0:CAP, cols] = dx[top, cols]

    def red_copy(d, m, s):
        cols = pl.ds(s * width, width)
        dev = ring_to[d]
        if m == 0:
            src, dst = yx.at[7, pl.ds((1 - d) * HALF, HALF), cols], f1.at[d, :, cols]
        elif m == 1:
            src, dst = yx.at[block(1 - d, 3), :, cols], f2.at[d, pl.ds(0, SLOTS), cols]
        elif m == 2:
            src, dst = f1.at[d, :, cols], f2.at[d, pl.ds(SLOTS, HALF), cols]
        else:
            src, dst = sx.at[d, m - 3, :, cols], rx.at[d, m - 3, :, cols]
            if m == 3 + d:
                dev = ring_x[d]
        return remote(src, dst, red_s.at[d, m, s], red_r.at[d, m, s], dev)

    def redp_copy(d, m):
        return remote(sp.at[d, m - 1], rpp.at[d, m - 1], redp_s.at[d, m - 1], redp_r.at[d, m - 1], ring_to[d])

    def back_landed(b, x):
        for i in back_routes(b, x):
            back_copy(b, i, x).wait_recv()

    def prob_part(b):
        oh0, oh1 = matches(gm[b], slot_names(z, SLOTS, 0))
        val = yp[b]
        p0 = jnp.sum(jnp.where(oh0, val, 0.0), axis=0, keepdims=True)
        p1 = jnp.sum(jnp.where(oh1, val, 0.0), axis=0, keepdims=True)
        return jnp.concatenate([p0, p1, jnp.zeros((6, ROWS), F32)], axis=0)

    def prob_stage(m):
        for d in range(2):
            if m == 1 and d == 1:
                continue
            b = block(1 - d, 5 - m)
            back_landed(b, 1)
            val = prob_part(b)
            if m > 2 or (m == 2 and d == 0):
                redp_copy(d, m - 1).wait_recv()
                val = val + rpp[d, m - 2]
            sp[d, m - 1] = val
            send(redp_copy(d, m))

    def spread_rows(hot, rows):
        return lax.dot_general(hot, rows, TN, preferred_element_type=F32)

    tile = 256
    pieces = d_model // tile // PARTS
    out_half = ((wg.at[:, pl.ds(0, hid)], wrg, og_out), (wu.at[:, pl.ds(0, hid)], wru, ou_out), (wd.at[pl.ds(0, hid)], wrd, od_out))

    def grad_gate_up(part):
        @pl.loop(part * pieces, (part + 1) * pieces)
        def _(n):
            at = pl.ds(pl.multiple_of(n * tile, tile), tile)
            tok = rt[:, at]
            for acts, other, mine in ((a_gate, wg, og_out), (a_up, wu, ou_out)):
                out = lax.dot_general(tok, acts[...], TN, preferred_element_type=F32).astype(BF16)
                mine[at, :] = out[:, 0:hid]
                other[at, 0:hid] = out[:, hid:full]

    def grad_down(part):
        @pl.loop(part * pieces, (part + 1) * pieces)
        def _(n):
            at = pl.ds(pl.multiple_of(n * tile, tile), tile)
            out = lax.dot_general(a_act[...], rg[:, at], TN, preferred_element_type=F32).astype(BF16)
            od_out[:, at] = out[0:hid, :]
            wd[0:hid, at] = out[hid:full, :]

    def wx_copy(j):
        return remote(out_half[j][0], out_half[j][1], wx_s.at[j], wx_r.at[j], twin)

    def finish_weight(j):
        wx_copy(j).wait_recv()
        _, got, mine = out_half[j]
        step = mine.shape[0] // 4

        @pl.loop(0, 4)
        def _(n):
            at = pl.ds(pl.multiple_of(n * step, step), step)
            mine[at, :] = (mine[at, :].astype(F32) + got[at, :].astype(F32)).astype(BF16)

    for s in range(PARTS):
        for b in (7, 5, 6):
            for i in range(1, NY):
                part_copy(b, i, s).wait_recv()
            if b == 7:
                for d in range(2):
                    send(red_copy(d, 0, s))
            else:
                send(red_copy(6 - b, 1, s))
        if s in (1, 3):
            prob_stage((s + 1) // 2)
        if s > 0:
            for d in range(2):
                red_copy(d, 0, s - 1).wait_recv()
                send(red_copy(d, 2, s - 1))
        if s == PARTS - 1:
            for d in range(2):
                red_copy(d, 0, s).wait_recv()
                send(red_copy(d, 2, s))
        grad_gate_up(s)
    send(wx_copy(0))
    send(wx_copy(1))
    for d in range(2):
        back_landed(block(1 - d, 2), 0)
    for s in range(PARTS):
        cols = slice(s * width, (s + 1) * width)
        for d in range(2):
            b = block(1 - d, 2)
            part = spread_rows(near_hot(gm[b]), yx[b, :, cols])
            red_copy(d, 1, s).wait_recv()
            red_copy(d, 2, s).wait_recv()
            part = part + spread_rows(far_hot(1 - d), f2[d, :, cols])
            sx[d, 0, :, cols] = part.astype(BF16)
            send(red_copy(d, 3, s))
        if s == 1:
            prob_stage(3)
        grad_down(s)
    send(wx_copy(2))
    for j in range(2):
        metax_copy(j).wait_recv()
    for d in range(2):
        back_landed(block(1 - d, 1), 0)
    for s in range(PARTS):
        cols = slice(s * width, (s + 1) * width)
        for d in range(2):
            b = block(1 - d, 1)
            meta = gmx[1] if d == 0 else gm[b]
            part = spread_rows(near_hot(meta), yx[b, :, cols])
            red_copy(d, 3, s).wait_recv()
            sx[d, 1, :, cols] = (part + rx[d, 0, :, cols].astype(F32)).astype(BF16)
            send(red_copy(d, 4, s))
        if s == 1:
            prob_stage(4)
        if s < 3:
            finish_weight(s)
    back_landed(0, 0)
    back_landed(0, 1)
    for s in range(PARTS):
        cols = slice(s * width, (s + 1) * width)
        part = spread_rows(near_hot(gmx[0]), yx[0, :, cols])
        for d in range(2):
            red_copy(d, 4, s).wait_recv()
        part = part + rx[0, 1, :, cols].astype(F32) + rx[1, 1, :, cols].astype(F32)
        gi_out[:, cols] = part.astype(BF16)
    for d in range(2):
        redp_copy(d, 4).wait_recv()
    pg_out[...] = (prob_part(0) + rpp[0, 3] + rpp[1, 3])[0:2, :]
    for copy in pending:
        copy.wait_send()


def per_device(tokens, out_grad, expert_ids, route_probs, gate_weight, up_weight, down_weight):
    rows, d_model = tokens.shape[1:]
    hid = gate_weight.shape[3]
    full = 2 * hid
    vmem = pltpu.VMEM
    dma = pltpu.SemaphoreType.DMA
    in_vmem = pl.BlockSpec(memory_space=pltpu.VMEM)
    anywhere = pl.BlockSpec(memory_space=pl.ANY)
    n_slots = NZ * SLOTS
    scratch = [
        vmem((rows, d_model), BF16), vmem((rows, d_model), BF16),
        vmem((4, ROWS, d_model), BF16), vmem((4, ROWS, d_model), BF16), vmem((8, 8, ROWS), F32), vmem((2, 8, ROWS), F32),
        vmem((8, SLOTS, d_model), BF16), vmem((8, SLOTS, d_model), BF16), vmem((8, SLOTS, ROWS), F32),
        vmem((2, 2, FAR, d_model), BF16), vmem((2, 2, FAR, d_model), BF16),
        vmem((n_slots, d_model), BF16), vmem((n_slots, d_model), BF16), vmem((n_slots, ROWS), F32),
        vmem((d_model, full), BF16), vmem((d_model, full), BF16), vmem((full, d_model), BF16),
        vmem((full, d_model), BF16), vmem((full, d_model), BF16), vmem((d_model, full), BF16),
        vmem((LAST, full), F32), vmem((LAST, full), F32),
        vmem((n_slots, full), BF16), vmem((n_slots, full), BF16), vmem((n_slots, full), BF16),
        vmem((n_slots, d_model), BF16), vmem((n_slots, ROWS), F32),
        vmem((8, SLOTS, d_model), BF16), vmem((8, SLOTS, ROWS), F32),
        vmem((2, HALF, d_model), BF16), vmem((2, FAR, d_model), BF16),
        vmem((2, 2, ROWS, d_model), BF16), vmem((2, 2, ROWS, d_model), BF16),
        vmem((2, 4, 8, ROWS), F32), vmem((2, 4, 8, ROWS), F32),
        vmem((d_model, hid), BF16), vmem((d_model, hid), BF16), vmem((hid, d_model), BF16),
        dma((2, 2, 4)), dma((2, 2, 4)), dma((2, 4)), dma((2, 4)), dma((2,)), dma((2,)),
        dma((8, 3, 3)), dma((8, 3, 3)), dma((8, 4, 2)), dma((8, 4, 2)), dma((3, 3, PARTS)), dma((3, 3, PARTS)),
        dma((2, 5, PARTS)), dma((2, 5, PARTS)), dma((2, 4)), dma((2, 4)),
        dma((2,)), dma((3,)), dma((3,)), dma((3,)), dma((3,)), dma((3,)),
    ]
    shapes = (
        jax.ShapeDtypeStruct((rows, d_model), BF16), jax.ShapeDtypeStruct((2, rows), F32),
        jax.ShapeDtypeStruct((d_model, hid), BF16), jax.ShapeDtypeStruct((d_model, hid), BF16),
        jax.ShapeDtypeStruct((hid, d_model), BF16))
    grad_in, prob, grad_gate, grad_up, grad_down = pl.pallas_call(
        kernel,
        out_shape=tuple(vmem(shape.shape, shape.dtype) for shape in shapes),
        in_specs=[in_vmem, in_vmem] + [anywhere] * 5,
        out_specs=(in_vmem,) * 5,
        scratch_shapes=scratch,
        compiler_params=pltpu.CompilerParams(
            collective_id=0, has_side_effects=True, vmem_limit_bytes=57 * 1024 * 1024),
    )(expert_ids[0].T, route_probs[0].T, tokens[0], out_grad[0], gate_weight[0, 0], up_weight[0, 0], down_weight[0, 0])
    return (
        grad_in[None], prob.T[None], grad_gate[None, None], grad_up[None, None], grad_down[None, None])


def solution(mesh):
    in_specs = (
        P("section", ("dp", "expert"), None), P("section", ("dp", "expert"), None),
        P("section", ("dp", "expert"), None), P("section", ("dp", "expert"), None),
        P("section", "expert", None, "dp"), P("section", "expert", None, "dp"), P("section", "expert", "dp", None))
    out_specs = (
        P("section", ("dp", "expert"), None), P("section", ("dp", "expert"), None),
        P("section", "expert", None, "dp"), P("section", "expert", None, "dp"), P("section", "expert", "dp", None))
    return jax.shard_map(per_device, mesh=mesh, in_specs=in_specs, out_specs=out_specs, check_vma=False)
```

```python
import jax
import jax.numpy as jnp
from jax import lax
from jax.experimental import pallas as pl
from jax.experimental.pallas import tpu as pltpu
from jax.sharding import PartitionSpec as P

MESH = pl.DeviceIdType.MESH
NY = 4
NZ = 8
CAP = 16
ROWS = 128
SLOTS = NY * CAP
HALF = SLOTS // 2
FAR = SLOTS + HALF
LAST = 3 * SLOTS
PARTS = 4
F32 = jnp.float32
BF16 = jnp.bfloat16
NT = (((1,), (1,)), ((), ()))
TN = (((0,), (0,)), ((), ()))


def block(direction, distance):
    if distance == 0:
        return 0
    if distance == 4:
        return 7
    return 2 * distance - 1 + direction


AHEAD = (0, block(1, 1))


def kernel(
    ids_ref, probs_ref, t_hbm, g_hbm, wg_hbm, wu_hbm, wd_hbm,
    gi_out, pg_out, og_out, ou_out, od_out,
    t_ref, g_ref, gt, gg, gm, gmx, tp, gp, pp, fs, fr, rt, rg, rp, wg, wu, wd,
    wgt, wut, wdt,
    z_gate, z_up, a_gate, a_up, a_act, dx, pr, yx, yp, f2, sx, rx, sp, rpp,
    wrg, wru, wrd,
    ring_s, ring_r, near_s, near_r, half_s, half_r, meta_s, meta_r, mx_s, mx_r, disp_s, disp_r, back_s, back_r, part_s, part_r,
    red_s, red_r, redp_s, redp_r, x_l, w_l, w_s, w_r, wx_s, wx_r,
):
    d_model = t_hbm.shape[1]
    hid = wg_hbm.shape[1]
    full = 2 * hid
    me = lax.axis_index("expert")
    core = lax.axis_index("dp")
    sec = lax.axis_index("section")
    n_sec = lax.axis_size("section")
    y = lax.rem(me, NY)
    z = me // NY
    x_prev = lax.rem(sec + n_sec - 1, n_sec)
    x_next = lax.rem(sec + 1, n_sec)
    ring = (lax.rem(z + 1, NZ) * NY + y, lax.rem(z + NZ - 1, NZ) * NY + y)
    column = [z * NY + lax.rem(y + i, NY) for i in range(NY)]
    ring_to = [{"expert": e} for e in ring]
    ring_two = [{"expert": lax.rem(z + 2, NZ) * NY + y}, {"expert": lax.rem(z + NZ - 2, NZ) * NY + y}]
    ring_x = [{"section": x_prev, "expert": e} for e in ring]
    y_to = [{"expert": e} for e in column]
    y_x = [{"section": x_prev, "expert": e} for e in column]
    twin = {"dp": 1 - core}
    pending = []

    def remote(src, dst, ssem, rsem, dev):
        return pltpu.make_async_remote_copy(
            src_ref=src, dst_ref=dst, send_sem=ssem, recv_sem=rsem, device_id=dev, device_id_type=MESH)

    def send(copy):
        copy.start()
        pending.append(copy)

    barrier = pltpu.get_barrier_semaphore()
    greet = ring_to + ring_two + y_to[1:] + [twin] + y_x + ring_x
    greet += [{"section": x_next, "expert": e} for e in column + list(ring)]
    for dev in greet:
        pl.semaphore_signal(barrier, inc=1, device_id=dev, device_id_type=MESH)

    local_w = [
        pltpu.make_async_copy(wg_hbm, wg.at[:, pl.ds(0, hid)], w_l.at[0]),
        pltpu.make_async_copy(wu_hbm, wu.at[:, pl.ds(0, hid)], w_l.at[1]),
        pltpu.make_async_copy(wd_hbm, wd.at[pl.ds(0, hid)], w_l.at[2]),
    ]
    for copy in local_w:
        copy.start()

    local_x = [pltpu.make_async_copy(t_hbm, t_ref, x_l.at[0]), pltpu.make_async_copy(g_hbm, g_ref, x_l.at[1])]
    for copy in local_x:
        copy.start()

    pl.semaphore_wait(barrier, len(greet))

    def meta_copy(d, k):
        src = gm.at[0] if k == 1 else gm.at[block(d, k - 1)]
        return remote(src, gm.at[block(d, k)], meta_s.at[d, k - 1], meta_r.at[d, k - 1], ring_to[d])

    def metax_copy(j):
        return remote(gm.at[AHEAD[j]], gmx.at[j], mx_s.at[j], mx_r.at[j], {"section": x_prev})

    def ring_copy(x, d, k):
        own, held, staged = ((t_hbm, gt, tp), (g_hbm, gg, gp))[x]
        if k == 1:
            src, dst = own, held.at[block(d, 1) - 1]
        elif k == 2:
            src, dst = held.at[block(d, 1) - 1], held.at[block(d, 2) - 1]
        else:
            src, dst = fs.at[x, d, pl.ds(SLOTS, HALF)], staged.at[7, pl.ds(d * HALF, HALF)]
        return remote(
            src, dst, ring_s.at[x, d, k - 1], ring_r.at[x, d, k - 1], ring_two[d] if k == 3 else ring_to[d])

    half_width = d_model // 2

    def near_copy(x, d, h):
        cols = pl.ds(h * half_width, half_width)
        return remote(
            fs.at[x, d, pl.ds(0, SLOTS), cols], fr.at[x, d, pl.ds(0, SLOTS), cols],
            near_s.at[x, d, h], near_r.at[x, d, h], ring_to[d])

    for d in range(2):
        send(ring_copy(0, d, 1))

    ids = ids_ref[...].astype(F32)
    experts = lax.broadcasted_iota(jnp.int32, (NY * NZ, ROWS), 0).astype(F32)
    hit0 = jnp.where(experts == ids[0:1, :], 1.0, 0.0)
    hit1 = jnp.where(experts == ids[1:2, :], 1.0, 0.0)
    earlier = jnp.where(
        lax.broadcasted_iota(jnp.int32, (ROWS, ROWS), 0) < lax.broadcasted_iota(jnp.int32, (ROWS, ROWS), 1), 1.0, 0.0
    ).astype(BF16)
    before = jnp.dot((hit0 + hit1).astype(BF16), earlier, preferred_element_type=F32)
    slot0 = ids[0:1, :] * CAP + jnp.sum(hit0 * before, axis=0, keepdims=True)
    slot1 = ids[1:2, :] * CAP + jnp.sum(hit1 * before, axis=0, keepdims=True)
    gm[0] = jnp.concatenate([slot0, slot1, probs_ref[...], jnp.zeros((4, ROWS), F32)], axis=0)

    for d in range(2):
        send(meta_copy(d, 1))
    for d in range(2):
        send(ring_copy(1, d, 1))
    send(metax_copy(0))
    w_copies = [
        remote(wg_hbm, wg.at[:, pl.ds(hid, hid)], w_s.at[0], w_r.at[0], twin),
        remote(wu_hbm, wu.at[:, pl.ds(hid, hid)], w_s.at[1], w_r.at[1], twin),
        remote(wd_hbm, wd.at[pl.ds(hid, hid)], w_s.at[2], w_r.at[2], twin),
    ]
    for copy in w_copies:
        send(copy)

    def slot_names(plane, rows, first):
        row = lax.broadcasted_iota(jnp.int32, (rows, ROWS), 0)
        return ((plane * NY + lax.rem(y + first + row // CAP, NY)) * CAP + lax.rem(row, CAP)).astype(F32)

    def matches(meta, names):
        return meta[0:1, :] == names, meta[1:2, :] == names

    def as_hot(pair):
        return (jnp.where(pair[0], 1.0, 0.0) + jnp.where(pair[1], 1.0, 0.0)).astype(BF16)

    def near_hot(meta):
        return as_hot(matches(meta, slot_names(z, SLOTS, 0)))

    def far_hot(d):
        step = 1 if d == 0 else NZ - 1
        names = jnp.concatenate([
            slot_names(lax.rem(z + step, NZ), SLOTS, 0), slot_names(lax.rem(z + 2 * step, NZ), HALF, 2 * d)], axis=0)
        return as_hot(matches(gm[block(d, 2)], names))

    def staged_at(b, x):
        if x == 2:
            return pp.at[b]
        if b in (5, 6):
            return fr.at[x, b - 5]
        return (tp, gp)[x].at[b]

    def disp_copy(b, i, x):
        landing = (rt, rg, rp)[x]
        src = staged_at(b, x).at[pl.ds(i * CAP, CAP)]
        dst = landing.at[pl.ds(b * SLOTS + (NY - i) * CAP, CAP)]
        return remote(src, dst, disp_s.at[b, i - 1, x], disp_r.at[b, i - 1, x], y_to[i])

    def pack(b, x):
        top = slice(b * SLOTS, b * SLOTS + CAP)
        if x == 2:
            meta = gm[b]
            oh0, oh1 = matches(meta, slot_names(z, SLOTS, 0))
            chosen = jnp.where(oh0, meta[2:3, :], 0.0) + jnp.where(oh1, meta[3:4, :], 0.0)
            spread = jnp.broadcast_to(jnp.sum(chosen, axis=1, keepdims=True), (SLOTS, ROWS))
            pp[b] = spread
            rp[top, :] = spread[0:CAP, :]
        elif b < 5:
            own, held, staged, landing = ((t_ref, gt, tp, rt), (g_ref, gg, gp, rg))[x]
            rows = own[...] if b == 0 else held[b - 1]
            packed = jnp.dot(near_hot(gm[b]), rows, preferred_element_type=F32).astype(BF16)
            staged[b] = packed
            landing[top, :] = packed[0:CAP, :]
        for i in range(1, NY):
            send(disp_copy(b, i, x))
        if x < 2 and b >= 5:
            (rt, rg)[x][top, :] = staged_at(b, x)[0:CAP, :]

    def half_copy(b, i, h):
        cols = pl.ds(h * half_width, half_width)
        return remote(
            fr.at[1, b - 5, pl.ds(i * CAP, CAP), cols], rg.at[pl.ds(b * SLOTS + (NY - i) * CAP, CAP), cols],
            half_s.at[b - 5, i - 1, h], half_r.at[b - 5, i - 1, h], y_to[i])

    def pack_half(d, h):
        near_copy(1, d, h).wait_recv()
        b = block(d, 3)
        for i in range(1, NY):
            send(half_copy(b, i, h))
        cols = slice(h * half_width, (h + 1) * half_width)
        rg[b * SLOTS:b * SLOTS + CAP, cols] = fr[1, d, 0:CAP, cols]

    def landed(b, x):
        for i in range(1, NY):
            if x == 1 and b in (5, 6):
                for h in range(2):
                    half_copy(b, i, h).wait_recv()
            else:
                disp_copy(b, i, x).wait_recv()

    def back_copy(b, i, x):
        rows = pl.ds(b * SLOTS + (0 if i == 0 else NY - i) * CAP, CAP)
        src, dst = ((dx, yx), (pr, yp))[x]
        dev = y_x[(NY - i) % NY] if x == 0 and b in AHEAD else y_to[(NY - i) % NY]
        return remote(src.at[rows], dst.at[b, pl.ds(i * CAP, CAP)], back_s.at[b, i, x], back_r.at[b, i, x], dev)

    def back_routes(b, x):
        return range(0 if x == 0 and b in AHEAD else 1, NY)

    def gate_up(first, count):
        tile = 256
        rows = pl.ds(first, count)

        @pl.loop(0, full // tile)
        def _(n):
            cols = pl.ds(pl.multiple_of(n * tile, tile), tile)
            tok = rt[rows, :]
            z_gate[0:count, cols] = jnp.dot(tok, wg[:, cols], preferred_element_type=F32)
            z_up[0:count, cols] = jnp.dot(tok, wu[:, cols], preferred_element_type=F32)

    def activations(first, count):
        tile = 256
        rows = pl.ds(first, count)
        pr[rows, :] = jnp.zeros((count, ROWS), F32)

        @pl.loop(0, full // tile)
        def _(n):
            cols = pl.ds(pl.multiple_of(n * tile, tile), tile)
            hidden = jnp.dot(rg[rows, :], wdt[:, cols], preferred_element_type=F32)
            gate = z_gate[0:count, cols]
            up = z_up[0:count, cols]
            prob = rp[rows, :][:, 0:1]
            sig = jax.nn.sigmoid(gate)
            silu = gate * sig
            act = silu * up
            a_act[rows, cols] = (prob * act).astype(BF16)
            pr[rows, :] += jnp.broadcast_to(jnp.sum(act * hidden, axis=1, keepdims=True), (count, ROWS))
            scaled = prob * hidden
            a_gate[rows, cols] = (scaled * up * sig * (1.0 + gate * (1.0 - sig))).astype(BF16)
            a_up[rows, cols] = (scaled * silu).astype(BF16)

    width = d_model // PARTS

    def dx_part(first, count, part):
        rows = pl.ds(first, count)
        cols = pl.ds(part * width, width) if isinstance(part, int) else pl.ds(pl.multiple_of(part * width, width), width)
        out = jnp.dot(a_gate[rows, :], wgt[:, cols], preferred_element_type=F32)
        out += jnp.dot(a_up[rows, :], wut[:, cols], preferred_element_type=F32)
        dx[rows, cols] = out.astype(BF16)

    def part_copy(b, i, part):
        cols = pl.ds(part * width, width)
        return remote(
            dx.at[pl.ds(b * SLOTS + (NY - i) * CAP, CAP), cols], yx.at[b, pl.ds(i * CAP, CAP), cols],
            part_s.at[b - 5, i - 1, part], part_r.at[b - 5, i - 1, part], y_to[NY - i])

    def send_back(blocks):
        for b in blocks:
            for x in range(2):
                for i in back_routes(b, x):
                    send(back_copy(b, i, x))
        for b in blocks:
            top = slice(b * SLOTS, b * SLOTS + CAP)
            if b not in AHEAD:
                yx[b, 0:CAP, :] = dx[top, :]
            yp[b, 0:CAP, :] = pr[top, :]

    def chunk(blocks):
        first, count = blocks[0] * SLOTS, len(blocks) * SLOTS
        for b in blocks:
            for x in (0, 1, 2):
                landed(b, x)
        gate_up(first, count)
        activations(first, count)

        @pl.loop(0, PARTS)
        def _(part):
            dx_part(first, count, part)

        send_back(blocks)

    for copy in local_x:
        copy.wait()
    for x in (2, 0, 1):
        pack(0, x)
    for d in range(2):
        meta_copy(d, 1).wait_recv()
        send(meta_copy(d, 2))
    for x in range(2):
        for d in range(2):
            ring_copy(x, d, 1).wait_recv()
            send(ring_copy(x, d, 2))
    send(metax_copy(1))
    for d in range(2):
        for x in (2, 0, 1):
            pack(block(d, 1), x)
    for copy in local_w:
        copy.wait()
    for copy in w_copies:
        copy.wait_recv()

    @pl.loop(0, full // 256)
    def _(n):
        at = pl.ds(pl.multiple_of(n * 256, 256), 256)
        wdt[:, at] = wd[at, :].T

    @pl.loop(0, d_model // 256)
    def _(n):
        at = pl.ds(pl.multiple_of(n * 256, 256), 256)
        wgt[:, at] = wg[at, :].T
        wut[:, at] = wu[at, :].T

    for d in range(2):
        meta_copy(d, 2).wait_recv()
        send(meta_copy(d, 3))
    for x in range(2):
        for d in range(2):
            ring_copy(x, d, 2).wait_recv()
            held = (gt, gg)[x]
            fs[x, d] = jnp.dot(far_hot(d), held[block(d, 2) - 1], preferred_element_type=F32).astype(BF16)
            send(ring_copy(x, d, 3))
            for h in range(2):
                send(near_copy(x, d, h))
        for d in range(2):
            if x == 0:
                pack(block(d, 2), 2)
            pack(block(d, 2), x)
        if x == 0:
            chunk((0, 1, 2))
    for d in range(2):
        meta_copy(d, 3).wait_recv()
        if d == 0:
            send(meta_copy(d, 4))
    for d in range(2):
        for h in range(2):
            near_copy(0, d, h).wait_recv()
        pack(block(d, 3), 0)
    for d in range(2):
        ring_copy(0, d, 3).wait_recv()
    pack(7, 0)
    for d in range(2):
        pack(block(d, 3), 2)
    chunk((3, 4))
    meta_copy(0, 4).wait_recv()
    pack(7, 2)
    for d in range(2):
        ring_copy(1, d, 3).wait_recv()
    pack(7, 1)
    for d in range(2):
        pack_half(d, 0)
    for b in (5, 6, 7):
        landed(b, 0)
    gate_up(5 * SLOTS, LAST)
    for d in range(2):
        pack_half(d, 1)
    for b in (5, 6, 7):
        landed(b, 1)
        landed(b, 2)
    activations(5 * SLOTS, LAST)
    for b in (7, 5, 6):
        for i in range(1, NY):
            send(back_copy(b, i, 1))
        yp[b, 0:CAP, :] = pr[b * SLOTS:b * SLOTS + CAP, :]
    for part in range(PARTS):
        dx_part(5 * SLOTS, LAST, part)
        for b in (7, 5, 6):
            for i in range(1, NY):
                send(part_copy(b, i, part))
        for b in (7, 5, 6):
            top, cols = slice(b * SLOTS, b * SLOTS + CAP), slice(part * width, (part + 1) * width)
            yx[b, 0:CAP, cols] = dx[top, cols]

    def red_copy(d, m, s):
        cols = pl.ds(s * width, width)
        dev = ring_to[d]
        if m == 0:
            src, dst = yx.at[7, pl.ds((1 - d) * HALF, HALF), cols], f2.at[d, pl.ds(SLOTS, HALF), cols]
            dev = ring_two[d]
        elif m == 1:
            src, dst = yx.at[block(1 - d, 3), :, cols], f2.at[d, pl.ds(0, SLOTS), cols]
        else:
            src, dst = sx.at[d, m - 3, :, cols], rx.at[d, m - 3, :, cols]
            if m == 3 + d:
                dev = ring_x[d]
        return remote(src, dst, red_s.at[d, m, s], red_r.at[d, m, s], dev)

    def redp_copy(d, m):
        return remote(sp.at[d, m - 1], rpp.at[d, m - 1], redp_s.at[d, m - 1], redp_r.at[d, m - 1], ring_to[d])

    def back_landed(b, x):
        for i in back_routes(b, x):
            back_copy(b, i, x).wait_recv()

    def prob_part(b):
        oh0, oh1 = matches(gm[b], slot_names(z, SLOTS, 0))
        val = yp[b]
        p0 = jnp.sum(jnp.where(oh0, val, 0.0), axis=0, keepdims=True)
        p1 = jnp.sum(jnp.where(oh1, val, 0.0), axis=0, keepdims=True)
        return jnp.concatenate([p0, p1, jnp.zeros((6, ROWS), F32)], axis=0)

    def prob_stage(m):
        for d in range(2):
            if m == 1 and d == 1:
                continue
            b = block(1 - d, 5 - m)
            back_landed(b, 1)
            val = prob_part(b)
            if m > 2 or (m == 2 and d == 0):
                redp_copy(d, m - 1).wait_recv()
                val = val + rpp[d, m - 2]
            sp[d, m - 1] = val
            send(redp_copy(d, m))

    def spread_rows(hot, rows):
        return lax.dot_general(hot, rows, TN, preferred_element_type=F32)

    tile = 256
    pieces = d_model // tile // PARTS
    out_half = ((wg.at[:, pl.ds(0, hid)], wrg, og_out), (wu.at[:, pl.ds(0, hid)], wru, ou_out), (wd.at[pl.ds(0, hid)], wrd, od_out))

    def grad_gate_up(part):
        @pl.loop(part * pieces, (part + 1) * pieces)
        def _(n):
            at = pl.ds(pl.multiple_of(n * tile, tile), tile)
            tok = rt[:, at]
            for acts, other, mine in ((a_gate, wg, og_out), (a_up, wu, ou_out)):
                out = lax.dot_general(tok, acts[...], TN, preferred_element_type=F32).astype(BF16)
                mine[at, :] = out[:, 0:hid]
                other[at, 0:hid] = out[:, hid:full]

    def grad_down(part):
        @pl.loop(part * pieces, (part + 1) * pieces)
        def _(n):
            at = pl.ds(pl.multiple_of(n * tile, tile), tile)
            out = lax.dot_general(a_act[...], rg[:, at], TN, preferred_element_type=F32).astype(BF16)
            od_out[:, at] = out[0:hid, :]
            wd[0:hid, at] = out[hid:full, :]

    def wx_copy(j):
        return remote(out_half[j][0], out_half[j][1], wx_s.at[j], wx_r.at[j], twin)

    def finish_weight(j):
        wx_copy(j).wait_recv()
        _, got, mine = out_half[j]
        step = mine.shape[0] // 4

        @pl.loop(0, 4)
        def _(n):
            at = pl.ds(pl.multiple_of(n * step, step), step)
            mine[at, :] = (mine[at, :].astype(F32) + got[at, :].astype(F32)).astype(BF16)

    for s in range(PARTS):
        for b in (7, 5, 6):
            for i in range(1, NY):
                part_copy(b, i, s).wait_recv()
            if b == 7:
                for d in range(2):
                    send(red_copy(d, 0, s))
            else:
                send(red_copy(6 - b, 1, s))
        if s in (1, 3):
            prob_stage((s + 1) // 2)
        grad_gate_up(s)
    send(wx_copy(0))
    send(wx_copy(1))
    for d in range(2):
        back_landed(block(1 - d, 2), 0)
    for s in range(PARTS):
        cols = slice(s * width, (s + 1) * width)
        for d in range(2):
            b = block(1 - d, 2)
            part = spread_rows(near_hot(gm[b]), yx[b, :, cols])
            red_copy(d, 1, s).wait_recv()
            red_copy(d, 0, s).wait_recv()
            part = part + spread_rows(far_hot(1 - d), f2[d, :, cols])
            sx[d, 0, :, cols] = part.astype(BF16)
            send(red_copy(d, 3, s))
        if s == 1:
            prob_stage(3)
        grad_down(s)
    send(wx_copy(2))
    for j in range(2):
        metax_copy(j).wait_recv()
    for d in range(2):
        back_landed(block(1 - d, 1), 0)
    for s in range(PARTS):
        cols = slice(s * width, (s + 1) * width)
        for d in range(2):
            b = block(1 - d, 1)
            meta = gmx[1] if d == 0 else gm[b]
            part = spread_rows(near_hot(meta), yx[b, :, cols])
            red_copy(d, 3, s).wait_recv()
            sx[d, 1, :, cols] = (part + rx[d, 0, :, cols].astype(F32)).astype(BF16)
            send(red_copy(d, 4, s))
        if s == 1:
            prob_stage(4)
        if s < 3:
            finish_weight(s)
    back_landed(0, 0)
    back_landed(0, 1)
    for s in range(PARTS):
        cols = slice(s * width, (s + 1) * width)
        part = spread_rows(near_hot(gmx[0]), yx[0, :, cols])
        for d in range(2):
            red_copy(d, 4, s).wait_recv()
        part = part + rx[0, 1, :, cols].astype(F32) + rx[1, 1, :, cols].astype(F32)
        gi_out[:, cols] = part.astype(BF16)
    for d in range(2):
        redp_copy(d, 4).wait_recv()
    pg_out[...] = (prob_part(0) + rpp[0, 3] + rpp[1, 3])[0:2, :]
    for copy in pending:
        copy.wait_send()


def hand_over(gi, pg, og, ou, od, gi_out, pg_out, og_out, ou_out, od_out, sems):
    pairs = ((og, og_out), (ou, ou_out), (od, od_out), (gi, gi_out), (pg, pg_out))
    copies = [pltpu.make_async_copy(src, dst, sems.at[j]) for j, (src, dst) in enumerate(pairs)]
    for copy in copies:
        copy.start()
    for copy in copies:
        copy.wait()


def per_device(tokens, out_grad, expert_ids, route_probs, gate_weight, up_weight, down_weight):
    rows, d_model = tokens.shape[1:]
    hid = gate_weight.shape[3]
    full = 2 * hid
    vmem = pltpu.VMEM
    dma = pltpu.SemaphoreType.DMA
    in_vmem = pl.BlockSpec(memory_space=pltpu.VMEM)
    anywhere = pl.BlockSpec(memory_space=pl.ANY)
    n_slots = NZ * SLOTS
    scratch = [
        vmem((rows, d_model), BF16), vmem((rows, d_model), BF16),
        vmem((4, ROWS, d_model), BF16), vmem((4, ROWS, d_model), BF16), vmem((8, 8, ROWS), F32), vmem((2, 8, ROWS), F32),
        vmem((8, SLOTS, d_model), BF16), vmem((8, SLOTS, d_model), BF16), vmem((8, SLOTS, ROWS), F32),
        vmem((2, 2, FAR, d_model), BF16), vmem((2, 2, SLOTS, d_model), BF16),
        vmem((n_slots, d_model), BF16), vmem((n_slots, d_model), BF16), vmem((n_slots, ROWS), F32),
        vmem((d_model, full), BF16), vmem((d_model, full), BF16), vmem((full, d_model), BF16),
        vmem((full, d_model), BF16), vmem((full, d_model), BF16), vmem((d_model, full), BF16),
        vmem((LAST, full), F32), vmem((LAST, full), F32),
        vmem((n_slots, full), BF16), vmem((n_slots, full), BF16), vmem((n_slots, full), BF16),
        vmem((n_slots, d_model), BF16), vmem((n_slots, ROWS), F32),
        vmem((8, SLOTS, d_model), BF16), vmem((8, SLOTS, ROWS), F32),
        vmem((2, FAR, d_model), BF16),
        vmem((2, 2, ROWS, d_model), BF16), vmem((2, 2, ROWS, d_model), BF16),
        vmem((2, 4, 8, ROWS), F32), vmem((2, 4, 8, ROWS), F32),
        vmem((d_model, hid), BF16), vmem((d_model, hid), BF16), vmem((hid, d_model), BF16),
        dma((2, 2, 3)), dma((2, 2, 3)), dma((2, 2, 2)), dma((2, 2, 2)), dma((2, 3, 2)), dma((2, 3, 2)),
        dma((2, 4)), dma((2, 4)), dma((2,)), dma((2,)),
        dma((8, 3, 3)), dma((8, 3, 3)), dma((8, 4, 2)), dma((8, 4, 2)), dma((3, 3, PARTS)), dma((3, 3, PARTS)),
        dma((2, 5, PARTS)), dma((2, 5, PARTS)), dma((2, 4)), dma((2, 4)),
        dma((2,)), dma((3,)), dma((3,)), dma((3,)), dma((3,)), dma((3,)),
    ]
    shapes = (
        jax.ShapeDtypeStruct((rows, d_model), BF16), jax.ShapeDtypeStruct((2, rows), F32),
        jax.ShapeDtypeStruct((d_model, hid), BF16), jax.ShapeDtypeStruct((d_model, hid), BF16),
        jax.ShapeDtypeStruct((hid, d_model), BF16))
    results = pl.pallas_call(
        kernel,
        out_shape=tuple(vmem(shape.shape, shape.dtype) for shape in shapes),
        in_specs=[in_vmem, in_vmem] + [anywhere] * 5,
        out_specs=(in_vmem,) * 5,
        scratch_shapes=scratch,
        compiler_params=pltpu.CompilerParams(
            collective_id=0, has_side_effects=True, vmem_limit_bytes=57 * 1024 * 1024),
    )(expert_ids[0].T, route_probs[0].T, tokens[0], out_grad[0], gate_weight[0, 0], up_weight[0, 0], down_weight[0, 0])
    grad_in, prob, grad_gate, grad_up, grad_down = pl.pallas_call(
        hand_over,
        out_shape=shapes,
        in_specs=[in_vmem] * 5,
        out_specs=(anywhere,) * 5,
        scratch_shapes=[dma((5,))],
        compiler_params=pltpu.CompilerParams(vmem_limit_bytes=1024 * 1024),
    )(*[pltpu.with_memory_space_constraint(result, pltpu.VMEM) for result in results])
    return (
        grad_in[None], prob.T[None], grad_gate[None, None], grad_up[None, None], grad_down[None, None])


def solution(mesh):
    in_specs = (
        P("section", ("dp", "expert"), None), P("section", ("dp", "expert"), None),
        P("section", ("dp", "expert"), None), P("section", ("dp", "expert"), None),
        P("section", "expert", None, "dp"), P("section", "expert", None, "dp"), P("section", "expert", "dp", None))
    out_specs = (
        P("section", ("dp", "expert"), None), P("section", ("dp", "expert"), None),
        P("section", "expert", None, "dp"), P("section", "expert", None, "dp"), P("section", "expert", "dp", None))
    return jax.shard_map(per_device, mesh=mesh, in_specs=in_specs, out_specs=out_specs, check_vma=False)
```

```python
import jax
import jax.numpy as jnp
from jax import lax
from jax.experimental import pallas as pl
from jax.experimental.pallas import tpu as pltpu
from jax.sharding import PartitionSpec as P

MESH = pl.DeviceIdType.MESH
NY = 4
NZ = 8
CAP = 16
ROWS = 128
SLOTS = NY * CAP
HALF = SLOTS // 2
FAR = SLOTS + HALF
LAST = 3 * SLOTS
PARTS = 4
F32 = jnp.float32
BF16 = jnp.bfloat16
NT = (((1,), (1,)), ((), ()))
TN = (((0,), (0,)), ((), ()))


def block(direction, distance):
    if distance == 0:
        return 0
    if distance == 4:
        return 7
    return 2 * distance - 1 + direction


AHEAD = (0, block(1, 1))


def kernel(
    ids_ref, probs_ref, t_hbm, g_hbm, wg_hbm, wu_hbm, wd_hbm,
    gi_out, pg_out, og_out, ou_out, od_out,
    t_ref, g_ref, gt, gg, gm, gmx, tp, gp, pp, fs, fr, rt, rg, rp, wg, wu, wd,
    wgt, wut, wdt,
    z_gate, z_up, a_gate, a_up, a_act, dx, pr, yx, yp, f2, sx, rx, sp, rpp,
    wrg, wru, wrd,
    ring_s, ring_r, near_s, near_r, half_s, half_r, meta_s, meta_r, mx_s, mx_r, disp_s, disp_r, back_s, back_r, part_s, part_r,
    red_s, red_r, redp_s, redp_r, x_l, w_l, w_s, w_r, wx_s, wx_r,
):
    d_model = t_hbm.shape[1]
    hid = wg_hbm.shape[1]
    full = 2 * hid
    me = lax.axis_index("expert")
    core = lax.axis_index("dp")
    sec = lax.axis_index("section")
    n_sec = lax.axis_size("section")
    y = lax.rem(me, NY)
    z = me // NY
    x_prev = lax.rem(sec + n_sec - 1, n_sec)
    x_next = lax.rem(sec + 1, n_sec)
    ring = (lax.rem(z + 1, NZ) * NY + y, lax.rem(z + NZ - 1, NZ) * NY + y)
    column = [z * NY + lax.rem(y + i, NY) for i in range(NY)]
    ring_to = [{"expert": e} for e in ring]
    ring_two = [{"expert": lax.rem(z + 2, NZ) * NY + y}, {"expert": lax.rem(z + NZ - 2, NZ) * NY + y}]
    ring_x = [{"section": x_prev, "expert": e} for e in ring]
    planes = [[lax.rem(z + h, NZ), lax.rem(z + NZ - h, NZ)] for h in range(3)]
    aslant = [[[{"expert": planes[h][d] * NY + lax.rem(y + i, NY)} for i in range(NY)] for d in range(2)] for h in range(3)]
    y_to = [{"expert": e} for e in column]
    y_x = [{"section": x_prev, "expert": e} for e in column]
    twin = {"dp": 1 - core}
    pending = []

    def remote(src, dst, ssem, rsem, dev):
        return pltpu.make_async_remote_copy(
            src_ref=src, dst_ref=dst, send_sem=ssem, recv_sem=rsem, device_id=dev, device_id_type=MESH)

    def send(copy):
        copy.start()
        pending.append(copy)

    barrier = pltpu.get_barrier_semaphore()
    greet = aslant[1][0] + aslant[1][1] + aslant[2][0] + aslant[2][1] + y_to[1:] + [twin] + y_x + ring_x
    greet += [{"section": x_next, "expert": e} for e in column + list(ring)]
    for dev in greet:
        pl.semaphore_signal(barrier, inc=1, device_id=dev, device_id_type=MESH)

    local_w = [
        pltpu.make_async_copy(wg_hbm, wg.at[:, pl.ds(0, hid)], w_l.at[0]),
        pltpu.make_async_copy(wu_hbm, wu.at[:, pl.ds(0, hid)], w_l.at[1]),
        pltpu.make_async_copy(wd_hbm, wd.at[pl.ds(0, hid)], w_l.at[2]),
    ]
    for copy in local_w:
        copy.start()

    local_x = [pltpu.make_async_copy(t_hbm, t_ref, x_l.at[0]), pltpu.make_async_copy(g_hbm, g_ref, x_l.at[1])]
    for copy in local_x:
        copy.start()

    pl.semaphore_wait(barrier, len(greet))

    def meta_copy(d, k):
        src = gm.at[0] if k == 1 else gm.at[block(d, k - 1)]
        return remote(src, gm.at[block(d, k)], meta_s.at[d, k - 1], meta_r.at[d, k - 1], ring_to[d])

    def metax_copy(j):
        return remote(gm.at[AHEAD[j]], gmx.at[j], mx_s.at[j], mx_r.at[j], {"section": x_prev})

    def ring_copy(x, d, k):
        own, held, staged = ((t_hbm, gt, tp), (g_hbm, gg, gp))[x]
        if k == 1:
            src, dst = own, held.at[block(d, 1) - 1]
        elif k == 2:
            src, dst = held.at[block(d, 1) - 1], held.at[block(d, 2) - 1]
        else:
            src, dst = fs.at[x, d, pl.ds(SLOTS, HALF)], staged.at[7, pl.ds(d * HALF, HALF)]
        return remote(
            src, dst, ring_s.at[x, d, k - 1], ring_r.at[x, d, k - 1], ring_two[d] if k == 3 else ring_to[d])

    half_width = d_model // 2

    def near_copy(x, d, h):
        cols = pl.ds(h * half_width, half_width)
        return remote(
            fs.at[x, d, pl.ds(0, SLOTS), cols], fr.at[x, d, pl.ds(0, SLOTS), cols],
            near_s.at[x, d, h], near_r.at[x, d, h], ring_to[d])

    for d in range(2):
        send(ring_copy(0, d, 1))

    ids = ids_ref[...].astype(F32)
    experts = lax.broadcasted_iota(jnp.int32, (NY * NZ, ROWS), 0).astype(F32)
    hit0 = jnp.where(experts == ids[0:1, :], 1.0, 0.0)
    hit1 = jnp.where(experts == ids[1:2, :], 1.0, 0.0)
    earlier = jnp.where(
        lax.broadcasted_iota(jnp.int32, (ROWS, ROWS), 0) < lax.broadcasted_iota(jnp.int32, (ROWS, ROWS), 1), 1.0, 0.0
    ).astype(BF16)
    before = jnp.dot((hit0 + hit1).astype(BF16), earlier, preferred_element_type=F32)
    slot0 = ids[0:1, :] * CAP + jnp.sum(hit0 * before, axis=0, keepdims=True)
    slot1 = ids[1:2, :] * CAP + jnp.sum(hit1 * before, axis=0, keepdims=True)
    gm[0] = jnp.concatenate([slot0, slot1, probs_ref[...], jnp.zeros((4, ROWS), F32)], axis=0)

    for d in range(2):
        send(meta_copy(d, 1))
    for d in range(2):
        send(ring_copy(1, d, 1))
    send(metax_copy(0))
    w_copies = [
        remote(wg_hbm, wg.at[:, pl.ds(hid, hid)], w_s.at[0], w_r.at[0], twin),
        remote(wu_hbm, wu.at[:, pl.ds(hid, hid)], w_s.at[1], w_r.at[1], twin),
        remote(wd_hbm, wd.at[pl.ds(hid, hid)], w_s.at[2], w_r.at[2], twin),
    ]
    for copy in w_copies:
        send(copy)

    def slot_names(plane, rows, first):
        row = lax.broadcasted_iota(jnp.int32, (rows, ROWS), 0)
        return ((plane * NY + lax.rem(y + first + row // CAP, NY)) * CAP + lax.rem(row, CAP)).astype(F32)

    def matches(meta, names):
        return meta[0:1, :] == names, meta[1:2, :] == names

    def as_hot(pair):
        return (jnp.where(pair[0], 1.0, 0.0) + jnp.where(pair[1], 1.0, 0.0)).astype(BF16)

    def near_hot(meta):
        return as_hot(matches(meta, slot_names(z, SLOTS, 0)))

    def far_hot(d):
        step = 1 if d == 0 else NZ - 1
        names = jnp.concatenate([
            slot_names(lax.rem(z + step, NZ), SLOTS, 0), slot_names(lax.rem(z + 2 * step, NZ), HALF, 2 * d)], axis=0)
        return as_hot(matches(gm[block(d, 2)], names))

    def staged_at(b, x):
        if x == 2:
            return pp.at[b]
        if b in (5, 6):
            return fr.at[x, b - 5]
        return (tp, gp)[x].at[b]

    def disp_copy(b, i, x):
        landing = (rt, rg, rp)[x]
        src = staged_at(b, x).at[pl.ds(i * CAP, CAP)]
        dst = landing.at[pl.ds(b * SLOTS + (NY - i) * CAP, CAP)]
        return remote(src, dst, disp_s.at[b, i - 1, x], disp_r.at[b, i - 1, x], y_to[i])

    def pack(b, x):
        top = slice(b * SLOTS, b * SLOTS + CAP)
        if x == 2:
            meta = gm[b]
            oh0, oh1 = matches(meta, slot_names(z, SLOTS, 0))
            chosen = jnp.where(oh0, meta[2:3, :], 0.0) + jnp.where(oh1, meta[3:4, :], 0.0)
            spread = jnp.broadcast_to(jnp.sum(chosen, axis=1, keepdims=True), (SLOTS, ROWS))
            pp[b] = spread
            rp[top, :] = spread[0:CAP, :]
        elif b < 5:
            own, held, staged, landing = ((t_ref, gt, tp, rt), (g_ref, gg, gp, rg))[x]
            rows = own[...] if b == 0 else held[b - 1]
            packed = jnp.dot(near_hot(gm[b]), rows, preferred_element_type=F32).astype(BF16)
            staged[b] = packed
            landing[top, :] = packed[0:CAP, :]
        for i in range(1, NY):
            send(disp_copy(b, i, x))
        if x < 2 and b >= 5:
            (rt, rg)[x][top, :] = staged_at(b, x)[0:CAP, :]

    def half_copy(b, i, h):
        cols = pl.ds(h * half_width, half_width)
        return remote(
            fr.at[1, b - 5, pl.ds(i * CAP, CAP), cols], rg.at[pl.ds(b * SLOTS + (NY - i) * CAP, CAP), cols],
            half_s.at[b - 5, i - 1, h], half_r.at[b - 5, i - 1, h], y_to[i])

    def pack_half(d, h):
        near_copy(1, d, h).wait_recv()
        b = block(d, 3)
        for i in range(1, NY):
            send(half_copy(b, i, h))
        cols = slice(h * half_width, (h + 1) * half_width)
        rg[b * SLOTS:b * SLOTS + CAP, cols] = fr[1, d, 0:CAP, cols]

    def landed(b, x):
        for i in range(1, NY):
            if x == 1 and b in (5, 6):
                for h in range(2):
                    half_copy(b, i, h).wait_recv()
            else:
                disp_copy(b, i, x).wait_recv()

    def back_copy(b, i, x):
        rows = pl.ds(b * SLOTS + (0 if i == 0 else NY - i) * CAP, CAP)
        src, dst = ((dx, yx), (pr, yp))[x]
        dev = y_x[(NY - i) % NY] if x == 0 and b in AHEAD else y_to[(NY - i) % NY]
        return remote(src.at[rows], dst.at[b, pl.ds(i * CAP, CAP)], back_s.at[b, i, x], back_r.at[b, i, x], dev)

    def back_routes(b, x):
        return range(0 if x == 0 and b in AHEAD else 1, NY)

    def gate_up(first, count):
        tile = 256
        rows = pl.ds(first, count)

        @pl.loop(0, full // tile)
        def _(n):
            cols = pl.ds(pl.multiple_of(n * tile, tile), tile)
            tok = rt[rows, :]
            z_gate[0:count, cols] = jnp.dot(tok, wg[:, cols], preferred_element_type=F32)
            z_up[0:count, cols] = jnp.dot(tok, wu[:, cols], preferred_element_type=F32)

    def activations(first, count):
        tile = 256
        rows = pl.ds(first, count)
        pr[rows, :] = jnp.zeros((count, ROWS), F32)

        @pl.loop(0, full // tile)
        def _(n):
            cols = pl.ds(pl.multiple_of(n * tile, tile), tile)
            hidden = jnp.dot(rg[rows, :], wdt[:, cols], preferred_element_type=F32)
            gate = z_gate[0:count, cols]
            up = z_up[0:count, cols]
            prob = rp[rows, :][:, 0:1]
            sig = jax.nn.sigmoid(gate)
            silu = gate * sig
            act = silu * up
            a_act[rows, cols] = (prob * act).astype(BF16)
            pr[rows, :] += jnp.broadcast_to(jnp.sum(act * hidden, axis=1, keepdims=True), (count, ROWS))
            scaled = prob * hidden
            a_gate[rows, cols] = (scaled * up * sig * (1.0 + gate * (1.0 - sig))).astype(BF16)
            a_up[rows, cols] = (scaled * silu).astype(BF16)

    width = d_model // PARTS

    def dx_part(first, count, part):
        rows = pl.ds(first, count)
        cols = pl.ds(part * width, width) if isinstance(part, int) else pl.ds(pl.multiple_of(part * width, width), width)
        out = jnp.dot(a_gate[rows, :], wgt[:, cols], preferred_element_type=F32)
        out += jnp.dot(a_up[rows, :], wut[:, cols], preferred_element_type=F32)
        dx[rows, cols] = out.astype(BF16)

    def part_copy(b, i, part):
        cols = pl.ds(part * width, width)
        q = (NY - i) % NY
        d, hops, row = (1 - i // 2, 2, NY + i % 2) if b == 7 else (6 - b, 1, i)
        return remote(
            dx.at[pl.ds(b * SLOTS + q * CAP, CAP), cols], f2.at[d, pl.ds(row * CAP, CAP), cols],
            part_s.at[b - 5, i, part], part_r.at[b - 5, i, part], aslant[hops][d][q])

    def send_back(blocks):
        for b in blocks:
            for x in range(2):
                for i in back_routes(b, x):
                    send(back_copy(b, i, x))
        for b in blocks:
            top = slice(b * SLOTS, b * SLOTS + CAP)
            if b not in AHEAD:
                yx[b, 0:CAP, :] = dx[top, :]
            yp[b, 0:CAP, :] = pr[top, :]

    def chunk(blocks):
        first, count = blocks[0] * SLOTS, len(blocks) * SLOTS
        for b in blocks:
            for x in (0, 1, 2):
                landed(b, x)
        gate_up(first, count)
        activations(first, count)

        @pl.loop(0, PARTS)
        def _(part):
            dx_part(first, count, part)

        send_back(blocks)

    for copy in local_x:
        copy.wait()
    for x in (2, 0, 1):
        pack(0, x)
    for d in range(2):
        meta_copy(d, 1).wait_recv()
        send(meta_copy(d, 2))
    for x in range(2):
        for d in range(2):
            ring_copy(x, d, 1).wait_recv()
            send(ring_copy(x, d, 2))
    send(metax_copy(1))
    for d in range(2):
        for x in (2, 0, 1):
            pack(block(d, 1), x)
    for copy in local_w:
        copy.wait()
    for copy in w_copies:
        copy.wait_recv()

    @pl.loop(0, full // 256)
    def _(n):
        at = pl.ds(pl.multiple_of(n * 256, 256), 256)
        wdt[:, at] = wd[at, :].T

    @pl.loop(0, d_model // 256)
    def _(n):
        at = pl.ds(pl.multiple_of(n * 256, 256), 256)
        wgt[:, at] = wg[at, :].T
        wut[:, at] = wu[at, :].T

    for d in range(2):
        meta_copy(d, 2).wait_recv()
        send(meta_copy(d, 3))
    for x in range(2):
        for d in range(2):
            ring_copy(x, d, 2).wait_recv()
            held = (gt, gg)[x]
            fs[x, d] = jnp.dot(far_hot(d), held[block(d, 2) - 1], preferred_element_type=F32).astype(BF16)
            send(ring_copy(x, d, 3))
            for h in range(2):
                send(near_copy(x, d, h))
        for d in range(2):
            if x == 0:
                pack(block(d, 2), 2)
            pack(block(d, 2), x)
        if x == 0:
            chunk((0, 1, 2))
    for d in range(2):
        meta_copy(d, 3).wait_recv()
        if d == 0:
            send(meta_copy(d, 4))
    for d in range(2):
        for h in range(2):
            near_copy(0, d, h).wait_recv()
        pack(block(d, 3), 0)
    for d in range(2):
        ring_copy(0, d, 3).wait_recv()
    pack(7, 0)
    for d in range(2):
        pack(block(d, 3), 2)
    chunk((3, 4))
    meta_copy(0, 4).wait_recv()
    pack(7, 2)
    for d in range(2):
        ring_copy(1, d, 3).wait_recv()
    pack(7, 1)
    for d in range(2):
        pack_half(d, 0)
    for b in (5, 6, 7):
        landed(b, 0)
    gate_up(5 * SLOTS, LAST)
    for d in range(2):
        pack_half(d, 1)
    for b in (5, 6, 7):
        landed(b, 1)
        landed(b, 2)
    activations(5 * SLOTS, LAST)
    for b in (7, 5, 6):
        for i in range(1, NY):
            send(back_copy(b, i, 1))
        yp[b, 0:CAP, :] = pr[b * SLOTS:b * SLOTS + CAP, :]
    for part in range(PARTS):
        dx_part(5 * SLOTS, LAST, part)
        for b in (7, 5, 6):
            for i in range(NY):
                send(part_copy(b, i, part))

    def red_copy(d, m, s):
        cols = pl.ds(s * width, width)
        dev = ring_to[d]
        src, dst = sx.at[d, m - 3, :, cols], rx.at[d, m - 3, :, cols]
        if m == 3 + d:
            dev = ring_x[d]
        return remote(src, dst, red_s.at[d, m - 3, s], red_r.at[d, m - 3, s], dev)

    def redp_copy(d, m):
        return remote(sp.at[d, m - 1], rpp.at[d, m - 1], redp_s.at[d, m - 1], redp_r.at[d, m - 1], ring_to[d])

    def back_landed(b, x):
        for i in back_routes(b, x):
            back_copy(b, i, x).wait_recv()

    def prob_part(b):
        oh0, oh1 = matches(gm[b], slot_names(z, SLOTS, 0))
        val = yp[b]
        p0 = jnp.sum(jnp.where(oh0, val, 0.0), axis=0, keepdims=True)
        p1 = jnp.sum(jnp.where(oh1, val, 0.0), axis=0, keepdims=True)
        return jnp.concatenate([p0, p1, jnp.zeros((6, ROWS), F32)], axis=0)

    def prob_stage(m):
        for d in range(2):
            if m == 1 and d == 1:
                continue
            b = block(1 - d, 5 - m)
            back_landed(b, 1)
            val = prob_part(b)
            if m > 2 or (m == 2 and d == 0):
                redp_copy(d, m - 1).wait_recv()
                val = val + rpp[d, m - 2]
            sp[d, m - 1] = val
            send(redp_copy(d, m))

    def spread_rows(hot, rows):
        return lax.dot_general(hot, rows, TN, preferred_element_type=F32)

    tile = 256
    pieces = d_model // tile // PARTS
    out_half = ((wg.at[:, pl.ds(0, hid)], wrg, og_out), (wu.at[:, pl.ds(0, hid)], wru, ou_out), (wd.at[pl.ds(0, hid)], wrd, od_out))

    def grad_gate_up(part):
        @pl.loop(part * pieces, (part + 1) * pieces)
        def _(n):
            at = pl.ds(pl.multiple_of(n * tile, tile), tile)
            tok = rt[:, at]
            for acts, other, mine in ((a_gate, wg, og_out), (a_up, wu, ou_out)):
                out = lax.dot_general(tok, acts[...], TN, preferred_element_type=F32).astype(BF16)
                mine[at, :] = out[:, 0:hid]
                other[at, 0:hid] = out[:, hid:full]

    def grad_down(part):
        @pl.loop(part * pieces, (part + 1) * pieces)
        def _(n):
            at = pl.ds(pl.multiple_of(n * tile, tile), tile)
            out = lax.dot_general(a_act[...], rg[:, at], TN, preferred_element_type=F32).astype(BF16)
            od_out[:, at] = out[0:hid, :]
            wd[0:hid, at] = out[hid:full, :]

    def wx_copy(j):
        return remote(out_half[j][0], out_half[j][1], wx_s.at[j], wx_r.at[j], twin)

    def finish_weight(j):
        wx_copy(j).wait_recv()
        _, got, mine = out_half[j]
        step = mine.shape[0] // 4

        @pl.loop(0, 4)
        def _(n):
            at = pl.ds(pl.multiple_of(n * step, step), step)
            mine[at, :] = (mine[at, :].astype(F32) + got[at, :].astype(F32)).astype(BF16)

    for s in range(PARTS):
        grad_gate_up(s)
        if s == 2:
            prob_stage(1)
    send(wx_copy(0))
    send(wx_copy(1))
    for d in range(2):
        back_landed(block(1 - d, 2), 0)
    for s in range(PARTS):
        cols = slice(s * width, (s + 1) * width)
        for d in range(2):
            b = block(1 - d, 2)
            part = spread_rows(near_hot(gm[b]), yx[b, :, cols])
            for c in range(NY):
                part_copy(6 - d, c, s).wait_recv()
            for c in (2 - 2 * d, 3 - 2 * d):
                part_copy(7, c, s).wait_recv()
            part = part + spread_rows(far_hot(1 - d), f2[d, :, cols])
            sx[d, 0, :, cols] = part.astype(BF16)
            send(red_copy(d, 3, s))
        if s == 3:
            prob_stage(2)
        grad_down(s)
    send(wx_copy(2))
    for j in range(2):
        metax_copy(j).wait_recv()
    for d in range(2):
        back_landed(block(1 - d, 1), 0)
    for s in range(PARTS):
        cols = slice(s * width, (s + 1) * width)
        for d in range(2):
            b = block(1 - d, 1)
            meta = gmx[1] if d == 0 else gm[b]
            part = spread_rows(near_hot(meta), yx[b, :, cols])
            red_copy(d, 3, s).wait_recv()
            sx[d, 1, :, cols] = (part + rx[d, 0, :, cols].astype(F32)).astype(BF16)
            send(red_copy(d, 4, s))
        if s in (2, 3):
            prob_stage(1 + s)
        if s < 3:
            finish_weight(s)
    back_landed(0, 0)
    back_landed(0, 1)
    for s in range(PARTS):
        cols = slice(s * width, (s + 1) * width)
        part = spread_rows(near_hot(gmx[0]), yx[0, :, cols])
        for d in range(2):
            red_copy(d, 4, s).wait_recv()
        part = part + rx[0, 1, :, cols].astype(F32) + rx[1, 1, :, cols].astype(F32)
        gi_out[:, cols] = part.astype(BF16)
    for d in range(2):
        redp_copy(d, 4).wait_recv()
    pg_out[...] = (prob_part(0) + rpp[0, 3] + rpp[1, 3])[0:2, :]
    for copy in pending:
        copy.wait_send()


def hand_over(gi, pg, og, ou, od, gi_out, pg_out, og_out, ou_out, od_out, sems):
    pairs = ((og, og_out), (ou, ou_out), (od, od_out), (gi, gi_out), (pg, pg_out))
    copies = [pltpu.make_async_copy(src, dst, sems.at[j]) for j, (src, dst) in enumerate(pairs)]
    for copy in copies:
        copy.start()
    for copy in copies:
        copy.wait()


def per_device(tokens, out_grad, expert_ids, route_probs, gate_weight, up_weight, down_weight):
    rows, d_model = tokens.shape[1:]
    hid = gate_weight.shape[3]
    full = 2 * hid
    vmem = pltpu.VMEM
    dma = pltpu.SemaphoreType.DMA
    in_vmem = pl.BlockSpec(memory_space=pltpu.VMEM)
    anywhere = pl.BlockSpec(memory_space=pl.ANY)
    n_slots = NZ * SLOTS
    scratch = [
        vmem((rows, d_model), BF16), vmem((rows, d_model), BF16),
        vmem((4, ROWS, d_model), BF16), vmem((4, ROWS, d_model), BF16), vmem((8, 8, ROWS), F32), vmem((2, 8, ROWS), F32),
        vmem((8, SLOTS, d_model), BF16), vmem((8, SLOTS, d_model), BF16), vmem((8, SLOTS, ROWS), F32),
        vmem((2, 2, FAR, d_model), BF16), vmem((2, 2, SLOTS, d_model), BF16),
        vmem((n_slots, d_model), BF16), vmem((n_slots, d_model), BF16), vmem((n_slots, ROWS), F32),
        vmem((d_model, full), BF16), vmem((d_model, full), BF16), vmem((full, d_model), BF16),
        vmem((full, d_model), BF16), vmem((full, d_model), BF16), vmem((d_model, full), BF16),
        vmem((LAST, full), F32), vmem((LAST, full), F32),
        vmem((n_slots, full), BF16), vmem((n_slots, full), BF16), vmem((n_slots, full), BF16),
        vmem((n_slots, d_model), BF16), vmem((n_slots, ROWS), F32),
        vmem((8, SLOTS, d_model), BF16), vmem((8, SLOTS, ROWS), F32),
        vmem((2, FAR, d_model), BF16),
        vmem((2, 2, ROWS, d_model), BF16), vmem((2, 2, ROWS, d_model), BF16),
        vmem((2, 4, 8, ROWS), F32), vmem((2, 4, 8, ROWS), F32),
        vmem((d_model, hid), BF16), vmem((d_model, hid), BF16), vmem((hid, d_model), BF16),
        dma((2, 2, 3)), dma((2, 2, 3)), dma((2, 2, 2)), dma((2, 2, 2)), dma((2, 3, 2)), dma((2, 3, 2)),
        dma((2, 4)), dma((2, 4)), dma((2,)), dma((2,)),
        dma((8, 3, 3)), dma((8, 3, 3)), dma((8, 4, 2)), dma((8, 4, 2)), dma((3, NY, PARTS)), dma((3, NY, PARTS)),
        dma((2, 2, PARTS)), dma((2, 2, PARTS)), dma((2, 4)), dma((2, 4)),
        dma((2,)), dma((3,)), dma((3,)), dma((3,)), dma((3,)), dma((3,)),
    ]
    shapes = (
        jax.ShapeDtypeStruct((rows, d_model), BF16), jax.ShapeDtypeStruct((2, rows), F32),
        jax.ShapeDtypeStruct((d_model, hid), BF16), jax.ShapeDtypeStruct((d_model, hid), BF16),
        jax.ShapeDtypeStruct((hid, d_model), BF16))
    results = pl.pallas_call(
        kernel,
        out_shape=tuple(vmem(shape.shape, shape.dtype) for shape in shapes),
        in_specs=[in_vmem, in_vmem] + [anywhere] * 5,
        out_specs=(in_vmem,) * 5,
        scratch_shapes=scratch,
        compiler_params=pltpu.CompilerParams(
            collective_id=0, has_side_effects=True, vmem_limit_bytes=57 * 1024 * 1024),
    )(expert_ids[0].T, route_probs[0].T, tokens[0], out_grad[0], gate_weight[0, 0], up_weight[0, 0], down_weight[0, 0])
    grad_in, prob, grad_gate, grad_up, grad_down = pl.pallas_call(
        hand_over,
        out_shape=shapes,
        in_specs=[in_vmem] * 5,
        out_specs=(anywhere,) * 5,
        scratch_shapes=[dma((5,))],
        compiler_params=pltpu.CompilerParams(vmem_limit_bytes=1024 * 1024),
    )(*[pltpu.with_memory_space_constraint(result, pltpu.VMEM) for result in results])
    return (
        grad_in[None], prob.T[None], grad_gate[None, None], grad_up[None, None], grad_down[None, None])


def solution(mesh):
    in_specs = (
        P("section", ("dp", "expert"), None), P("section", ("dp", "expert"), None),
        P("section", ("dp", "expert"), None), P("section", ("dp", "expert"), None),
        P("section", "expert", None, "dp"), P("section", "expert", None, "dp"), P("section", "expert", "dp", None))
    out_specs = (
        P("section", ("dp", "expert"), None), P("section", ("dp", "expert"), None),
        P("section", "expert", None, "dp"), P("section", "expert", None, "dp"), P("section", "expert", "dp", None))
    return jax.shard_map(per_device, mesh=mesh, in_specs=in_specs, out_specs=out_specs, check_vma=False)
```
